256 devices in a mesh: grid: 16 (over y, x), day: 16 (over z, core).
Axes of the slice: x: 4, y: 4, z: 8, core: 2. Of those that a mesh axis runs over, the one named last changes fastest.
Arguments:
- anomalies: bfloat16 [16384, 65536], P('day', 'grid'), may hold values from -6 to 6
- eofs: bfloat16 [64, 65536], P(None, ('grid', 'day')), may hold values from -0.0234375 to 0.0234375
- means_init: float32 [8, 64], replicated, may hold values from -4 to 4
- variances: float32 [8, 64], replicated, may hold values from 0.05 to 2
- mixing: float32 [8], replicated, may hold values from 0.5 to 2
Outputs:
- regime_means: float32 [8, 64], replicated
- regime_covs: float32 [8, 64, 64], replicated
- regime_weights: float32 [8], replicated
- membership: float32 [8, 16384], P(None, 'day')
- composites: bfloat16 [8, 65536], P(None, ('grid', 'day'))
The draws below stay inside these ranges and needn't reach their ends.
All inputs are finite; a program needn't handle non-finite values.
Results may differ from the reference program's by a relative error of at most 0.0034.
Values may be sent and summed in bfloat16 or wider, within the bound.
No kernel may reach another device: no remote copies, remote signals or barrier semaphores. Data moves between devices by JAX's collectives and lax.ppermute only.
A program may use at most 64 MiB of HBM per device.

```python
import math
import jax
import jax.numpy as jnp
from jax import lax

K = 64
R = 8
ITERS = 2
PIX = 65536
DAYS = 16384


def steps_of(key, extent, cuts, smallest, top_value):
    gain = 1.0
    for axis_at, blocks in cuts:
        heights = jax.random.uniform(jax.random.fold_in(jax.random.fold_in(key, 6), axis_at), (blocks,), jnp.float32, smallest / len(cuts), top_value / len(cuts))
        gain = gain * jnp.repeat(jnp.exp(heights), extent[axis_at] // blocks).reshape((-1,) + (1,) * (len(extent) - 1 - axis_at))
    return gain


def bell_draw(rng, dims, deviation, bound, shards=(), held_as=jnp.bfloat16):
    array = jax.random.normal(rng, dims, jnp.float32) * deviation
    if len(shards) > 0:
        array = steps_of(rng, dims, shards, -0.22, 0.18) * array
    return jnp.clip(array, min=-bound, max=bound).astype(held_as)


def setup_inputs(seed: int = 0) -> dict:
    key_of = jax.random.split(jax.random.key(seed), 6)
    return {
        "anomalies": bell_draw(key_of[0], (DAYS, PIX), 1.0, 6.0, ((0, 16), (1, 16))),
        "eofs": bell_draw(key_of[1], (K, PIX), PIX ** -0.5, 0.0234375, ((1, 256),)),
        "means_init": bell_draw(key_of[2], (R, K), 1.0, 4.0, (), jnp.float32),
        "variances": jnp.clip(jnp.exp(jax.random.uniform(key_of[3], (R, K), jnp.float32, math.log(0.05), math.log(2.0))), 0.05, 2.0),
        "mixing": jnp.clip(jax.random.uniform(key_of[4], (R,), jnp.float32, 0.5, 2.0), 0.5, 2.0),
    }


PRECISE = lax.Precision.HIGHEST
REG = 0.01

def log_density(pcs_t, means, covs, weights):
    regimes = means.shape[0]
    width = means.shape[1]
    eye = jnp.broadcast_to(jnp.eye(width, dtype=jnp.float32), (regimes, width, width))
    factor = jnp.linalg.cholesky(covs)
    inverse = lax.linalg.triangular_solve(factor, eye, left_side=True, lower=True)
    centred = pcs_t[None, :, :] - means[:, :, None]
    shifted = jnp.einsum('rkj,rjd->rkd', inverse, centred, precision=PRECISE)
    logdet = jnp.sum(jnp.log(jnp.diagonal(factor, axis1=1, axis2=2)), axis=1)
    return jnp.log(weights)[:, None] - logdet[:, None] - 0.5 * jnp.sum(shifted * shifted, axis=1)

def responsibilities(pcs_t, means, covs, weights):
    logp = log_density(pcs_t, means, covs, weights)
    top = jnp.max(logp, axis=0, keepdims=True)
    expo = jnp.exp(logp - top)
    return expo / jnp.sum(expo, axis=0, keepdims=True)

def second_moments(pcs_t, resp, means):
    diff = pcs_t[None, :, :] - means[:, :, None]
    return jnp.einsum('rkd,rjd->rkj', diff * resp[:, None, :], diff, precision=PRECISE)

def reference(anomalies, eofs, means_init, variances, mixing):
    pcs = lax.dot_general(anomalies.astype(jnp.float32), eofs.astype(jnp.float32), (((1,), (1,)), ((), ())), preferred_element_type=jnp.float32)
    pcs_t = pcs.T
    eye = jnp.eye(means_init.shape[1], dtype=jnp.float32)
    means = means_init
    covs = variances[:, :, None] * eye[None]
    weights = mixing / jnp.sum(mixing)
    for step in range(ITERS):
        resp = responsibilities(pcs_t, means, covs, weights)
        counted = jnp.maximum(jnp.sum(resp, axis=1), 1.0)
        means = lax.dot_general(resp, pcs_t, (((1,), (1,)), ((), ())), precision=PRECISE) / counted[:, None]
        covs = second_moments(pcs_t, resp, means) / counted[:, None, None] + REG * eye[None]
        weights = counted / jnp.sum(counted)
    member = responsibilities(pcs_t, means, covs, weights)
    counted = jnp.maximum(jnp.sum(member, axis=1), 1.0)
    sums = jnp.dot(member.astype(jnp.bfloat16).astype(jnp.float32), anomalies.astype(jnp.float32), preferred_element_type=jnp.float32)
    composites = (sums / counted[:, None]).astype(jnp.bfloat16)
    return (means, covs, weights, member, composites)
```

```python
import jax
import jax.numpy as jnp
from jax import lax
from jax.experimental import pallas as pl
from jax.experimental.pallas import tpu as pltpu
from jax.sharding import Mesh, PartitionSpec as P

ITERS = 2
K = 64
PRECISE = lax.Precision.HIGHEST
REG = 0.01
SWAP = [(0, 1), (1, 0)]


def lanes_of(x, index):
    return jnp.take_along_axis(x, index, axis=1)


def eliminate(groups):
    lane = lax.broadcasted_iota(jnp.int32, (8, 128), 1)
    sub = lax.broadcasted_iota(jnp.int32, (8, 128), 0)
    half = (lane >= K).astype(jnp.int32) * K
    col = lane - half
    for k in range(K):
        g, s = divmod(k, 8)
        row = jnp.broadcast_to(groups[g][s:s + 1, :], (8, 128))
        at = half + k
        pivot = lanes_of(row, at)
        scaled = jnp.where(col == k, 1.0, row) / pivot
        for i in range(g, 8):
            if i == g and s == 7:
                continue
            factor = lanes_of(groups[i], at)
            new = jnp.where(col == k, 0.0, groups[i]) - factor * scaled
            groups[i] = jnp.where(sub > s, new, groups[i]) if i == g else new
    outs = []
    logs = jnp.zeros((8, 128), jnp.float32)
    for i in range(8):
        row_id = sub + 8 * i
        diag = lanes_of(groups[i], half + row_id)
        unit = jnp.where(col < row_id, groups[i], jnp.where(col == row_id, 1.0, 0.0))
        outs.append(unit * lax.rsqrt(diag))
        logs = logs + jnp.log(diag)
    return outs, 0.5 * jnp.sum(logs, axis=0, keepdims=True)


def factor_kernel(covs_ref, inv_ref, logdet_ref):
    regimes = covs_ref.shape[0]
    for p in range(regimes // 2):
        both = jnp.concatenate([covs_ref[2 * p], covs_ref[2 * p + 1]], axis=1)
        groups = [both[8 * i:8 * i + 8] for i in range(8)]
        outs, logs = eliminate(groups)
        both = jnp.concatenate(outs, axis=0)
        inv_ref[2 * p] = both[:, :K]
        inv_ref[2 * p + 1] = both[:, K:]
        logdet_ref[2 * p:2 * p + 1, :] = jnp.broadcast_to(logs[:, 0:1], (1, 128))
        logdet_ref[2 * p + 1:2 * p + 2, :] = jnp.broadcast_to(logs[:, K:K + 1], (1, 128))


def factor(covs):
    regimes = covs.shape[0]
    vmem = pl.BlockSpec(memory_space=pltpu.VMEM)
    inverse, logdet = pl.pallas_call(
        factor_kernel,
        out_shape=(
            jax.ShapeDtypeStruct(covs.shape, jnp.float32),
            jax.ShapeDtypeStruct((regimes, 128), jnp.float32),
        ),
        in_specs=[vmem],
        out_specs=(vmem, vmem),
    )(covs)
    return inverse, logdet[:, 0]


def softmax_of(logp):
    top = jnp.max(logp, axis=0, keepdims=True)
    expo = jnp.exp(logp - top)
    return expo / jnp.sum(expo, axis=0, keepdims=True)


def first_step(centred, variances, weights):
    maha = jnp.sum(centred * centred / variances[:, :, None], axis=1)
    logdet = 0.5 * jnp.sum(jnp.log(variances), axis=1)
    return softmax_of(jnp.log(weights)[:, None] - logdet[:, None] - 0.5 * maha)


def later_step(centred, inverse, logdet, weights):
    shifted = jnp.einsum("rkj,rjd->rkd", inverse, centred, precision=PRECISE)
    return softmax_of(jnp.log(weights)[:, None] - logdet[:, None] - 0.5 * jnp.sum(shifted * shifted, axis=1))


def total(values):
    flat = values.reshape(-1, 128)
    flat = flat + lax.ppermute(flat, "core", SWAP)
    spread = jnp.broadcast_to(flat[None], (8,) + flat.shape)
    return jnp.sum(lax.all_to_all(spread, "z", 0, 0), axis=0).reshape(values.shape)


def update(centred, resp, means):
    regimes = means.shape[0]
    count = jnp.sum(resp, axis=1)
    first = jnp.einsum("rd,rkd->rk", resp, centred, precision=PRECISE)
    second = jnp.einsum("rkd,rjd->rkj", centred * resp[:, None, :], centred, precision=PRECISE)
    packed = jnp.concatenate(
        [second, first[:, None, :], jnp.broadcast_to(count[:, None, None], (regimes, 1, K))], axis=1)
    packed = total(packed)
    second, first, count = packed[:, :K], packed[:, K], packed[:, K + 1, 0]
    counted = jnp.maximum(count, 1.0)
    moved = (first + count[:, None] * means) / counted[:, None]
    delta = moved - means
    cross = first[:, :, None] * delta[:, None, :]
    second = second - cross - jnp.swapaxes(cross, 1, 2) + count[:, None, None] * delta[:, :, None] * delta[:, None, :]
    covs = second / counted[:, None, None] + REG * jnp.eye(K, dtype=jnp.float32)[None]
    return moved, covs, counted / jnp.sum(counted)


def body(anomalies, eofs, means_init, variances, mixing):
    core = lax.axis_index("core")
    own = lax.all_to_all(jnp.broadcast_to(eofs[None], (8,) + eofs.shape), "z", 0, 0)
    other = lax.ppermute(own, "core", SWAP)
    first = jnp.where(core == 0, own, other)
    second = jnp.where(core == 0, other, own)
    patterns = jnp.stack([first, second], axis=1)
    patterns = jnp.transpose(patterns, (2, 0, 1, 3)).reshape(K, -1)
    partial = lax.dot_general(
        patterns, anomalies, (((1,), (1,)), ((), ())), preferred_element_type=jnp.float32)
    days = anomalies.shape[0]
    blocks = lax.all_to_all(partial.reshape(16, K // 16, days), "grid", 0, 0)
    mine = jnp.sum(blocks, axis=0)
    pcs_t = lax.all_to_all(jnp.broadcast_to(mine[None], (16,) + mine.shape), "grid", 0, 0).reshape(K, days)

    means = means_init
    weights = mixing / jnp.sum(mixing)
    centred = pcs_t[None] - means[:, :, None]
    resp = first_step(centred, variances, weights)
    for step in range(ITERS):
        means, covs, weights = update(centred, resp, means)
        inverse, logdet = factor(covs)
        centred = pcs_t[None] - means[:, :, None]
        resp = later_step(centred, inverse, logdet, weights)
    member = resp
    terms = jnp.dot(member.astype(jnp.bfloat16), anomalies, preferred_element_type=jnp.float32)
    pixels = terms.shape[1] // 16
    terms = jnp.swapaxes(terms.reshape(8, 16, pixels), 0, 1)
    count = jnp.broadcast_to(jnp.sum(member, axis=1)[None, :, None], (16, 8, 128))
    got = jnp.sum(lax.all_to_all(jnp.concatenate([terms, count], axis=2), ("z", "core"), 0, 0), axis=0)
    counted = jnp.maximum(got[:, pixels:pixels + 1], 1.0)
    composites = (got[:, :pixels] / counted).astype(jnp.bfloat16)
    return (means, covs, weights, member, composites)


def solution(mesh):
    split = Mesh(mesh.devices.reshape(16, 8, 2), ("grid", "z", "core"))
    day = ("z", "core")
    in_specs = (P(day, "grid"), P(None, ("grid",) + day), P(), P(), P())
    out_specs = (P(), P(), P(), P(None, day), P(None, ("grid",) + day))
    return jax.shard_map(body, mesh=split, in_specs=in_specs, out_specs=out_specs, check_vma=False)
```

```python
import functools

import jax
import jax.numpy as jnp
from jax import lax
from jax.experimental import pallas as pl
from jax.experimental.pallas import tpu as pltpu
from jax.sharding import Mesh, PartitionSpec as P

K = 64
R = 8
HALF = R // 2
F32 = jnp.float32
BF16 = jnp.bfloat16
PRECISE = lax.Precision.HIGHEST
REG = 0.01
SWAP = [(0, 1), (1, 0)]
ROWS = K + 8
VMEM = pl.BlockSpec(memory_space=pltpu.VMEM)


def call(kernel, outs, operands, **cost):
    return pl.pallas_call(
        kernel,
        out_shape=tuple(jax.ShapeDtypeStruct(s, d) for s, d in outs),
        in_specs=[VMEM] * len(operands),
        out_specs=tuple([VMEM] * len(outs)),
        compiler_params=pltpu.CompilerParams(vmem_limit_bytes=48 * 1024 * 1024),
    )(*operands)


def lanes_of(x, index):
    return jnp.take_along_axis(x, index, axis=1)


def tile_ids():
    lane = lax.broadcasted_iota(jnp.int32, (8, 128), 1)
    sub = lax.broadcasted_iota(jnp.int32, (8, 128), 0)
    half = (lane >= K).astype(jnp.int32) * K
    return sub, half, lane - half


def by_core(core, at_zero, at_one):
    return jnp.where(core == 0, at_zero, at_one)


def eliminate(pairs):
    sub, half, col = tile_ids()
    for k in range(K):
        g, s = divmod(k, 8)
        at = half + k
        here = col == k
        for groups in pairs:
            row = jnp.broadcast_to(groups[g][s:s + 1, :], (8, 128))
            scaled = jnp.where(here, 1.0, row) / lanes_of(row, at)
            for i in range(g, 8):
                if i == g and s == 7:
                    continue
                new = jnp.where(here, 0.0, groups[i]) - lanes_of(groups[i], at) * scaled
                groups[i] = jnp.where(sub > s, new, groups[i]) if i == g else new
    results = []
    for groups in pairs:
        outs = []
        logs = jnp.zeros((8, 128), F32)
        for i in range(8):
            row_id = sub + 8 * i
            diag = lanes_of(groups[i], half + row_id)
            unit = jnp.where(col < row_id, groups[i], jnp.where(col == row_id, 1.0, 0.0))
            outs.append(unit * lax.rsqrt(diag))
            logs = logs + jnp.log(diag)
        results.append((outs, 0.5 * jnp.sum(logs, axis=0, keepdims=True)))
    return results


def project_kernel(own_ref, other_ref, fields_ref, out_ref):
    core = lax.axis_index("core")
    parts = []
    for z in range(8):
        own, other = own_ref[z], other_ref[z]
        parts += [by_core(core, own, other), by_core(core, other, own)]
    patterns = jnp.concatenate(parts, axis=1)
    for c in range(4):
        part = lax.dot_general(
            patterns, fields_ref[256 * c:256 * c + 256, :], (((1,), (1,)), ((), ())),
            preferred_element_type=F32)
        at = 256 * (c % 2)
        for b in range(8):
            out_ref[2 * b + c // 2, :, at:at + 256] = part[8 * b:8 * b + 8, :]


def read_pcs(pcs_ref):
    return [jnp.concatenate([pcs_ref[2 * b], pcs_ref[2 * b + 1]], axis=1) for b in range(8)]


def centre(pcs, row, offset):
    sub, _, _ = tile_ids()
    row = jnp.broadcast_to(row, (8, 128))
    outs = []
    for b in range(8):
        column = lanes_of(row, sub + (8 * b + offset))
        outs.append(pcs[b] - jnp.concatenate([column] * (pcs[b].shape[1] // 128), axis=1))
    return outs


def softmax_of(logp):
    top = jnp.max(logp, axis=0, keepdims=True)
    expo = jnp.exp(logp - top)
    return expo / jnp.sum(expo, axis=0, keepdims=True)


def moments(core, centred_of, resp, keep_ref, send_ref):
    days = resp.shape[1]
    counts = jnp.broadcast_to(jnp.sum(resp, axis=1, keepdims=True), (R, K))
    row_id = lax.broadcasted_iota(jnp.int32, (K, K), 0)
    col_id = lax.broadcasted_iota(jnp.int32, (K, K), 1)
    seconds, firsts = [], []
    for r in range(R):
        centred = jnp.concatenate(centred_of(r), axis=0)
        weight = resp[r:r + 1, :]
        left = jnp.concatenate([centred * weight, jnp.broadcast_to(weight, (8, days))], axis=0)
        got = lax.dot_general(left, centred, (((1,), (1,)), ((), ())), precision=PRECISE,
                              preferred_element_type=F32)
        seconds.append(got[:K])
        firsts.append(got[K:K + 1])
    packs = []
    for h in range(2):
        squares, tails = [], []
        for p in range(2):
            a = HALF * h + 2 * p
            squares.append(jnp.where(row_id >= col_id, seconds[a], seconds[a + 1]))
            diag = jnp.sum(jnp.where(row_id == col_id, seconds[a + 1], 0.0), axis=0, keepdims=True)
            tails.append(jnp.concatenate(
                [diag, firsts[a], firsts[a + 1], counts[a:a + 1], counts[a + 1:a + 2],
                 jnp.zeros((3, K), F32)], axis=0))
        packs.append(jnp.concatenate(
            [jnp.concatenate(squares, axis=1), jnp.concatenate(tails, axis=1)], axis=0))
    keep_ref[...] = by_core(core, packs[0], packs[1])
    send_ref[...] = by_core(core, packs[1], packs[0])


def first_kernel(pcs_ref, params_ref, base_ref, keep_ref, send_ref):
    pcs = read_pcs(pcs_ref)
    sub, _, _ = tile_ids()
    logs = []
    for r in range(R):
        row = params_ref[r:r + 1, :]
        inverse = jnp.broadcast_to(1.0 / row, (8, 128))
        centred = centre(pcs, row, 0)
        total = None
        for b in range(8):
            column = lanes_of(inverse, sub + (8 * b + K))
            scale = jnp.concatenate([column] * 8, axis=1)
            term = centred[b] * centred[b] * scale
            total = term if total is None else total + term
        logs.append(jnp.sum(total, axis=0, keepdims=True))
    logp = base_ref[:, 0:1] - 0.5 * jnp.concatenate(logs, axis=0)
    resp = softmax_of(logp)
    moments(lax.axis_index("core"), lambda r: centre(pcs, params_ref[r:r + 1, :], 0), resp, keep_ref, send_ref)


def merge_kernel(parts_ref, shift_ref, block_ref, covs_ref):
    sub, half, col = tile_ids()
    total = parts_ref[0]
    for z in range(1, 8):
        total = total + parts_ref[z]
    packed = total[:K]
    flipped = packed.T
    flipped = jnp.concatenate([flipped[:K], flipped[K:]], axis=1)
    tail = total[K:]
    pairs = []
    infos = []
    for p in range(2):
        first, count, shift = tail[1 + p:2 + p], tail[3 + p:4 + p], shift_ref[p:p + 1, :]
        counted = jnp.maximum(count, 1.0)
        mean = (first + count * shift) / counted
        delta = mean - shift
        rest = first - count * delta
        first_b, delta_b = jnp.broadcast_to(first, (8, 128)), jnp.broadcast_to(delta, (8, 128))
        scale = 1.0 / counted
        groups = []
        for g in range(8):
            row_id = sub + 8 * g
            straight, turned = packed[8 * g:8 * g + 8], flipped[8 * g:8 * g + 8]
            if p == 0:
                second = jnp.where(row_id >= col, straight, turned)
            else:
                second = jnp.where(row_id < col, straight, jnp.where(row_id > col, turned, tail[0:1]))
            at = half + row_id
            second = second - lanes_of(first_b, at) * delta - lanes_of(delta_b, at) * rest
            cov = second * scale + jnp.where(row_id == col, REG, 0.0)
            covs_ref[K * p + 8 * g:K * p + 8 * g + 8, :] = cov
            groups.append(cov)
        pairs.append(groups)
        infos.append((mean, counted))
    (first_out, first_log), (second_out, second_log) = eliminate(pairs)
    for g in range(8):
        block_ref[8 * g:8 * g + 8, :] = first_out[g]
        block_ref[K + 8 * g:K + 8 * g + 8, :] = second_out[g]
    block_ref[2 * K:, :] = jnp.concatenate(
        [infos[0][0], infos[1][0], first_log, second_log, infos[0][1], infos[1][1],
         jnp.zeros((2, 128), F32)], axis=0)


def regime_of(r):
    h, q = divmod(r, HALF)
    return h, q % 2, K * (q // 2)


def expect(pcs, halves):
    infos = [block[2 * K:] for block in halves]

    def column(at):
        rows = []
        for r in range(R):
            h, p, offset = regime_of(r)
            rows.append(infos[h][at + p:at + p + 1, offset:offset + 1])
        return jnp.concatenate(rows, axis=0)

    counted = column(4)
    weights = counted / jnp.sum(counted, axis=0, keepdims=True)
    logs = []
    for r in range(R):
        h, p, offset = regime_of(r)
        inverse = halves[h][K * p:K * p + K, offset:offset + K]
        centred = jnp.concatenate(centre(pcs, infos[h][p:p + 1, :], offset), axis=0)
        shifted = lax.dot_general(inverse, centred, (((1,), (0,)), ((), ())), precision=PRECISE,
                                  preferred_element_type=F32)
        logs.append(jnp.sum(shifted * shifted, axis=0, keepdims=True))
    logp = jnp.log(weights) - column(2) - 0.5 * jnp.concatenate(logs, axis=0)
    return softmax_of(logp), weights


def halves_of(core, keep_ref, got_ref):
    keep, got = keep_ref[...], got_ref[...]
    return [by_core(core, keep, got), by_core(core, got, keep)]


def middle_kernel(pcs_ref, keep_ref, got_ref, out_keep_ref, out_send_ref):
    core = lax.axis_index("core")
    pcs = read_pcs(pcs_ref)
    halves = halves_of(core, keep_ref, got_ref)
    resp, _ = expect(pcs, halves)

    def centred_of(r):
        h, p, offset = regime_of(r)
        return centre(pcs, halves[h][2 * K + p:2 * K + p + 1, :], offset)

    moments(core, centred_of, resp, out_keep_ref, out_send_ref)


def last_kernel(pcs_ref, keep_ref, got_ref, fields_ref, member_ref, terms_ref, means_ref, weights_ref):
    core = lax.axis_index("core")
    pcs = read_pcs(pcs_ref)
    halves = halves_of(core, keep_ref, got_ref)
    member, weights = expect(pcs, halves)
    member_ref[...] = member
    weights_ref[...] = jnp.broadcast_to(weights, (R, 128))
    means = []
    for r in range(R):
        h, p, offset = regime_of(r)
        means.append(halves[h][2 * K + p:2 * K + p + 1, offset:offset + K])
    means_ref[...] = jnp.concatenate(means, axis=0)
    count = jnp.broadcast_to(jnp.sum(member, axis=1, keepdims=True), (R, 128))
    rounded = member.astype(BF16)
    for j in range(16):
        terms_ref[j, :, 0:256] = jnp.dot(rounded, fields_ref[:, 256 * j:256 * j + 256], preferred_element_type=F32)
        terms_ref[j, :, 256:384] = count


def spread(x, n):
    return jnp.broadcast_to(x[None], (n,) + x.shape)


def merge(keep, send, shift):
    half = keep + lax.ppermute(send, "core", SWAP)
    parts = lax.all_to_all(spread(half, 8), "z", 0, 0)
    return call(merge_kernel, [((2 * K + 8, 128), F32), ((2 * K, 128), F32)], [parts, shift])


def body(anomalies, eofs, means_init, variances, mixing):
    days = anomalies.shape[0]
    core = lax.axis_index("core")
    own = lax.all_to_all(spread(eofs, 8), "z", 0, 0)
    other = lax.ppermute(own, "core", SWAP)
    partial, = call(project_kernel, [((16, 8, days // 2), F32)], [own, other, anomalies])
    mine = jnp.sum(lax.all_to_all(partial, "grid", 0, 0), axis=0)
    pcs = lax.all_to_all(spread(mine, 16), "grid", 0, 0)

    params = jnp.concatenate([means_init, variances], axis=1)
    base = jnp.log(mixing / jnp.sum(mixing)) - 0.5 * jnp.sum(jnp.log(variances), axis=1)
    base = jnp.broadcast_to(base[:, None], (R, 128))
    sides = means_init.reshape(2, 2, 2, K).swapaxes(1, 2).reshape(2, 2, 2 * K)
    shift = jnp.where(core == 0, sides[0], sides[1])

    pack = [((ROWS, 128), F32)] * 2
    keep, send = call(first_kernel, pack, [pcs, params, base])
    block, _ = merge(keep, send, shift)
    got = lax.ppermute(block, "core", SWAP)
    keep, send = call(middle_kernel, pack, [pcs, block, got])
    block, covs = merge(keep, send, block[2 * K:2 * K + 2])
    got = lax.ppermute(block, "core", SWAP)
    got_covs = lax.ppermute(covs, "core", SWAP)
    member, terms, means, weights = call(
        last_kernel,
        [((R, days), F32), ((16, R, 384), F32), ((R, K), F32), ((R, 128), F32)],
        [pcs, block, got, anomalies])
    sums = jnp.sum(lax.all_to_all(terms, ("z", "core"), 0, 0), axis=0)
    composites = (sums[:, :256] / jnp.maximum(sums[:, 256:257], 1.0)).astype(BF16)

    both = jnp.where(core == 0, jnp.stack([covs, got_covs]), jnp.stack([got_covs, covs]))
    covs = both.reshape(2, 2, K, 2, K).transpose(0, 3, 1, 2, 4).reshape(R, K, K)
    return (means, covs, weights[:, 0], member, composites)


def solution(mesh):
    split = Mesh(mesh.devices.reshape(16, 8, 2), ("grid", "z", "core"))
    day = ("z", "core")
    in_specs = (P(day, "grid"), P(None, ("grid",) + day), P(), P(), P())
    out_specs = (P(), P(), P(), P(None, day), P(None, ("grid",) + day))
    return jax.shard_map(body, mesh=split, in_specs=in_specs, out_specs=out_specs, check_vma=False)
```

```python
import functools

import jax
import jax.numpy as jnp
from jax import lax
from jax.experimental import pallas as pl
from jax.experimental.pallas import tpu as pltpu
from jax.sharding import Mesh, PartitionSpec as P

K = 64
R = 8
HALF = R // 2
F32 = jnp.float32
BF16 = jnp.bfloat16
PRECISE = lax.Precision.HIGHEST
REG = 0.01
SWAP = [(0, 1), (1, 0)]
ROWS = K + 8
LIMIT = 48 * 1024 * 1024
CHUNKS = 8
VMEM = pl.BlockSpec(memory_space=pltpu.VMEM)
HBM = pl.BlockSpec(memory_space=pltpu.HBM)


def call(kernel, outs, operands, scratch=(), stay=0):
    return pl.pallas_call(
        kernel,
        out_shape=tuple(jax.ShapeDtypeStruct(s, d) for s, d in outs),
        in_specs=[VMEM] * (len(operands) - stay) + [HBM] * stay,
        out_specs=tuple([VMEM] * len(outs)),
        scratch_shapes=scratch,
        compiler_params=pltpu.CompilerParams(vmem_limit_bytes=LIMIT),
    )(*operands)


def lanes_of(x, index):
    return jnp.take_along_axis(x, index, axis=1)


def tile_ids():
    lane = lax.broadcasted_iota(jnp.int32, (8, 128), 1)
    sub = lax.broadcasted_iota(jnp.int32, (8, 128), 0)
    half = (lane >= K).astype(jnp.int32) * K
    return sub, half, lane - half


def by_core(core, at_zero, at_one):
    return jnp.where(core == 0, at_zero, at_one)


def eliminate(pairs):
    sub, half, col = tile_ids()
    for k in range(0, K, 2):
        g, s = divmod(k, 8)
        at0, at1 = half + k, half + k + 1
        here0, here1 = col == k, col == k + 1
        here = here0 | here1
        for groups in pairs:
            row0 = jnp.broadcast_to(groups[g][s:s + 1, :], (8, 128))
            row1 = jnp.broadcast_to(groups[g][s + 1:s + 2, :], (8, 128))
            a, b, c = lanes_of(row0, at0), lanes_of(row0, at1), lanes_of(row1, at1)
            scale = 1.0 / (a * c - b * b)
            row0 = jnp.where(here, here0.astype(F32), row0) * scale
            row1 = jnp.where(here, here1.astype(F32), row1) * scale
            scaled0 = c * row0 - b * row1
            scaled1 = a * row1 - b * row0
            for i in range(g, 8):
                if i == g and s == 6:
                    continue
                f0, f1 = lanes_of(groups[i], at0), lanes_of(groups[i], at1)
                new = jnp.where(here, 0.0, groups[i]) - f0 * scaled0 - f1 * scaled1
                groups[i] = jnp.where(sub > s + 1, new, groups[i]) if i == g else new
    odd = (sub & 1) == 1
    results = []
    for groups in pairs:
        outs = []
        logs = jnp.zeros((8, 128), F32)
        for i in range(8):
            row_id = sub + 8 * i
            diag = lanes_of(groups[i], half + row_id)
            side = lanes_of(groups[i], half + (row_id ^ 1))
            unit = jnp.where(col < row_id - (sub & 1), groups[i], (col == row_id).astype(F32))
            ratio = side / pltpu.roll(diag, 1, 0)
            unit = jnp.where(odd, unit - ratio * pltpu.roll(unit, 1, 0), unit)
            diag = jnp.where(odd, diag - ratio * side, diag)
            outs.append(unit * lax.rsqrt(diag))
            logs = logs + jnp.log(diag)
        results.append((outs, 0.5 * jnp.sum(logs, axis=0, keepdims=True)))
    return results


def copies_of(fields_ref, out_ref, sems):
    rows = fields_ref.shape[0] // CHUNKS
    return [
        pltpu.make_async_copy(
            fields_ref.at[pl.ds(rows * i, rows)], out_ref.at[pl.ds(rows * i, rows)], sems.at[i])
        for i in range(CHUNKS)]


def project_kernel(own_ref, other_ref, fields_ref, out_ref, held_ref, sems):
    copies = copies_of(fields_ref, held_ref, sems)
    for copy in copies:
        copy.start()
    core = lax.axis_index("core")
    parts = []
    for z in range(8):
        own, other = own_ref[z], other_ref[z]
        parts += [by_core(core, own, other), by_core(core, other, own)]
    patterns = jnp.concatenate(parts, axis=1)
    for c in range(CHUNKS):
        copies[c].wait()
        part = lax.dot_general(
            held_ref[128 * c:128 * c + 128, :], patterns, (((1,), (1,)), ((), ())),
            preferred_element_type=F32).T
        at = 128 * (c % 4)
        for b in range(8):
            out_ref[2 * b + c // 4, :, at:at + 128] = part[8 * b:8 * b + 8, :]


def read_pcs(pcs_ref):
    return [jnp.concatenate([pcs_ref[2 * b], pcs_ref[2 * b + 1]], axis=1) for b in range(8)]


def centre(pcs, row, offset):
    sub, _, _ = tile_ids()
    row = jnp.broadcast_to(row, (8, 128))
    outs = []
    for b in range(8):
        column = lanes_of(row, sub + (8 * b + offset))
        outs.append(pcs[b] - jnp.concatenate([column] * (pcs[b].shape[1] // 128), axis=1))
    return outs


def softmax_of(logp):
    top = jnp.max(logp, axis=0, keepdims=True)
    expo = jnp.exp(logp - top)
    return expo / jnp.sum(expo, axis=0, keepdims=True)


def moments(core, centred_of, resp, keep_ref, send_ref):
    days = resp.shape[1]
    counts = jnp.broadcast_to(jnp.sum(resp, axis=1, keepdims=True), (R, K))
    row_id = lax.broadcasted_iota(jnp.int32, (K, K), 0)
    col_id = lax.broadcasted_iota(jnp.int32, (K, K), 1)
    seconds, firsts = [], []
    for r in range(R):
        centred = jnp.concatenate(centred_of(r), axis=0)
        weight = resp[r:r + 1, :]
        left = jnp.concatenate([centred * weight, jnp.broadcast_to(weight, (8, days))], axis=0)
        got = lax.dot_general(left, centred, (((1,), (1,)), ((), ())), precision=PRECISE,
                              preferred_element_type=F32)
        seconds.append(got[:K])
        firsts.append(got[K:K + 1])
    packs = []
    for h in range(2):
        squares, tails = [], []
        for p in range(2):
            a = HALF * h + 2 * p
            squares.append(jnp.where(row_id >= col_id, seconds[a], seconds[a + 1]))
            diag = jnp.sum(jnp.where(row_id == col_id, seconds[a + 1], 0.0), axis=0, keepdims=True)
            tails.append(jnp.concatenate(
                [diag, firsts[a], firsts[a + 1], counts[a:a + 1], counts[a + 1:a + 2],
                 jnp.zeros((3, K), F32)], axis=0))
        packs.append(jnp.concatenate(
            [jnp.concatenate(squares, axis=1), jnp.concatenate(tails, axis=1)], axis=0))
    keep_ref[...] = by_core(core, packs[0], packs[1])
    send_ref[...] = by_core(core, packs[1], packs[0])


def first_kernel(pcs_ref, params_ref, base_ref, keep_ref, send_ref):
    pcs = read_pcs(pcs_ref)
    sub, _, _ = tile_ids()
    logs = []
    for r in range(R):
        row = params_ref[r:r + 1, :]
        inverse = jnp.broadcast_to(1.0 / row, (8, 128))
        centred = centre(pcs, row, 0)
        total = None
        for b in range(8):
            column = lanes_of(inverse, sub + (8 * b + K))
            scale = jnp.concatenate([column] * 8, axis=1)
            term = centred[b] * centred[b] * scale
            total = term if total is None else total + term
        logs.append(jnp.sum(total, axis=0, keepdims=True))
    logp = base_ref[:, 0:1] - 0.5 * jnp.concatenate(logs, axis=0)
    resp = softmax_of(logp)
    moments(lax.axis_index("core"), lambda r: centre(pcs, params_ref[r:r + 1, :], 0), resp, keep_ref, send_ref)


def merge_kernel(parts_ref, shift_ref, block_ref, covs_ref):
    sub, half, col = tile_ids()
    total = parts_ref[0]
    for z in range(1, 8):
        total = total + parts_ref[z]
    packed = total[:K]
    flipped = packed.T
    flipped = jnp.concatenate([flipped[:K], flipped[K:]], axis=1)
    tail = total[K:]
    pairs = []
    infos = []
    for p in range(2):
        first, count, shift = tail[1 + p:2 + p], tail[3 + p:4 + p], shift_ref[p:p + 1, :]
        counted = jnp.maximum(count, 1.0)
        mean = (first + count * shift) / counted
        delta = mean - shift
        rest = first - count * delta
        first_b, delta_b = jnp.broadcast_to(first, (8, 128)), jnp.broadcast_to(delta, (8, 128))
        scale = 1.0 / counted
        groups = []
        for g in range(8):
            row_id = sub + 8 * g
            straight, turned = packed[8 * g:8 * g + 8], flipped[8 * g:8 * g + 8]
            if p == 0:
                second = jnp.where(row_id >= col, straight, turned)
            else:
                second = jnp.where(row_id < col, straight, jnp.where(row_id > col, turned, tail[0:1]))
            at = half + row_id
            second = second - lanes_of(first_b, at) * delta - lanes_of(delta_b, at) * rest
            cov = second * scale + jnp.where(row_id == col, REG, 0.0)
            covs_ref[K * p + 8 * g:K * p + 8 * g + 8, :] = cov
            groups.append(cov)
        pairs.append(groups)
        infos.append((mean, counted))
    (first_out, first_log), (second_out, second_log) = eliminate(pairs)
    for g in range(8):
        block_ref[8 * g:8 * g + 8, :] = first_out[g]
        block_ref[K + 8 * g:K + 8 * g + 8, :] = second_out[g]
    block_ref[2 * K:, :] = jnp.concatenate(
        [infos[0][0], infos[1][0], first_log, second_log, infos[0][1], infos[1][1],
         jnp.zeros((2, 128), F32)], axis=0)


def regime_of(r):
    h, q = divmod(r, HALF)
    return h, q % 2, K * (q // 2)


def expect(pcs, halves):
    infos = [block[2 * K:] for block in halves]

    def column(at):
        rows = []
        for r in range(R):
            h, p, offset = regime_of(r)
            rows.append(infos[h][at + p:at + p + 1, offset:offset + 1])
        return jnp.concatenate(rows, axis=0)

    counted = column(4)
    weights = counted / jnp.sum(counted, axis=0, keepdims=True)
    logs = []
    for r in range(R):
        h, p, offset = regime_of(r)
        inverse = halves[h][K * p:K * p + K, offset:offset + K]
        centred = jnp.concatenate(centre(pcs, infos[h][p:p + 1, :], offset), axis=0)
        shifted = lax.dot_general(inverse, centred, (((1,), (0,)), ((), ())), precision=PRECISE,
                                  preferred_element_type=F32)
        logs.append(jnp.sum(shifted * shifted, axis=0, keepdims=True))
    logp = jnp.log(weights) - column(2) - 0.5 * jnp.concatenate(logs, axis=0)
    return softmax_of(logp), weights


def halves_of(core, keep_ref, got_ref):
    keep, got = keep_ref[...], got_ref[...]
    return [by_core(core, keep, got), by_core(core, got, keep)]


def middle_kernel(pcs_ref, keep_ref, got_ref, out_keep_ref, out_send_ref):
    core = lax.axis_index("core")
    pcs = read_pcs(pcs_ref)
    halves = halves_of(core, keep_ref, got_ref)
    resp, _ = expect(pcs, halves)

    def centred_of(r):
        h, p, offset = regime_of(r)
        return centre(pcs, halves[h][2 * K + p:2 * K + p + 1, :], offset)

    moments(core, centred_of, resp, out_keep_ref, out_send_ref)


def last_kernel(pcs_ref, keep_ref, got_ref, fields_ref, member_ref, terms_ref, means_ref, weights_ref,
                held_ref, sems):
    copies = copies_of(fields_ref, held_ref, sems)
    for copy in copies:
        copy.start()
    core = lax.axis_index("core")
    pcs = read_pcs(pcs_ref)
    halves = halves_of(core, keep_ref, got_ref)
    member, weights = expect(pcs, halves)
    member_ref[...] = member
    weights_ref[...] = jnp.broadcast_to(weights, (R, 128))
    means = []
    for r in range(R):
        h, p, offset = regime_of(r)
        means.append(halves[h][2 * K + p:2 * K + p + 1, offset:offset + K])
    means_ref[...] = jnp.concatenate(means, axis=0)
    count = jnp.broadcast_to(jnp.sum(member, axis=1, keepdims=True), (R, 128))
    rounded = member.astype(BF16)
    for copy in copies:
        copy.wait()
    for j in range(16):
        terms_ref[j, :, 0:256] = jnp.dot(rounded, held_ref[:, 256 * j:256 * j + 256], preferred_element_type=F32)
        terms_ref[j, :, 256:384] = count


def spread(x, n):
    return jnp.broadcast_to(x[None], (n,) + x.shape)


def merge(keep, send, shift):
    half = keep + lax.ppermute(send, "core", SWAP)
    parts = lax.all_to_all(spread(half, 8), "z", 0, 0)
    return call(merge_kernel, [((2 * K + 8, 128), F32), ((2 * K, 128), F32)], [parts, shift])


def body(anomalies, eofs, means_init, variances, mixing):
    days = anomalies.shape[0]
    core = lax.axis_index("core")
    own = lax.all_to_all(spread(eofs, 8), "z", 0, 0)
    other = lax.ppermute(own, "core", SWAP)
    held = [pltpu.VMEM(anomalies.shape, anomalies.dtype), pltpu.SemaphoreType.DMA((CHUNKS,))]
    partial, = call(
        project_kernel, [((16, 8, days // 2), F32)], [own, other, anomalies], scratch=held, stay=1)
    mine = jnp.sum(lax.all_to_all(partial, "grid", 0, 0), axis=0)
    pcs = lax.all_to_all(spread(mine, 16), "grid", 0, 0)

    params = jnp.concatenate([means_init, variances], axis=1)
    base = jnp.log(mixing / jnp.sum(mixing)) - 0.5 * jnp.sum(jnp.log(variances), axis=1)
    base = jnp.broadcast_to(base[:, None], (R, 128))
    sides = means_init.reshape(2, 2, 2, K).swapaxes(1, 2).reshape(2, 2, 2 * K)
    shift = jnp.where(core == 0, sides[0], sides[1])

    pack = [((ROWS, 128), F32)] * 2
    keep, send = call(first_kernel, pack, [pcs, params, base])
    block, _ = merge(keep, send, shift)
    got = lax.ppermute(block, "core", SWAP)
    keep, send = call(middle_kernel, pack, [pcs, block, got])
    block, covs = merge(keep, send, block[2 * K:2 * K + 2])
    got = lax.ppermute(block, "core", SWAP)
    got_covs = lax.ppermute(covs, "core", SWAP)
    member, terms, means, weights = call(
        last_kernel,
        [((R, days), F32), ((16, R, 384), F32), ((R, K), F32), ((R, 128), F32)],
        [pcs, block, got, anomalies],
        scratch=held, stay=1)
    sums = jnp.sum(lax.all_to_all(terms, ("z", "core"), 0, 0), axis=0)
    composites = (sums[:, :256] / jnp.maximum(sums[:, 256:257], 1.0)).astype(BF16)

    both = jnp.where(core == 0, jnp.stack([covs, got_covs]), jnp.stack([got_covs, covs]))
    covs = both.reshape(2, 2, K, 2, K).transpose(0, 3, 1, 2, 4).reshape(R, K, K)
    return (means, covs, weights[:, 0], member, composites)


def solution(mesh):
    split = Mesh(mesh.devices.reshape(16, 8, 2), ("grid", "z", "core"))
    day = ("z", "core")
    in_specs = (P(day, "grid"), P(None, ("grid",) + day), P(), P(), P())
    out_specs = (P(), P(), P(), P(None, day), P(None, ("grid",) + day))
    return jax.shard_map(body, mesh=split, in_specs=in_specs, out_specs=out_specs, check_vma=False)
```

```python
import functools

import jax
import jax.numpy as jnp
from jax import lax
from jax.experimental import pallas as pl
from jax.experimental.pallas import tpu as pltpu
from jax.sharding import Mesh, PartitionSpec as P

K = 64
R = 8
HALF = R // 2
F32 = jnp.float32
BF16 = jnp.bfloat16
PRECISE = lax.Precision.HIGHEST
REG = 0.01
SWAP = [(0, 1), (1, 0)]
ROWS = K + 8
LIMIT = 48 * 1024 * 1024
SMALL = 16 * 1024 * 1024
COVER = pl.CostEstimate(flops=20 * 10 ** 10, transcendentals=0, bytes_accessed=0)
VMEM = pl.BlockSpec(memory_space=pltpu.VMEM)


def call(kernel, outs, operands, limit=LIMIT, cost=None):
    return pl.pallas_call(
        kernel,
        out_shape=tuple(jax.ShapeDtypeStruct(s, d) for s, d in outs),
        in_specs=[VMEM] * len(operands),
        out_specs=tuple([VMEM] * len(outs)),
        compiler_params=pltpu.CompilerParams(vmem_limit_bytes=limit),
        cost_estimate=cost,
    )(*operands)


def lanes_of(x, index):
    return jnp.take_along_axis(x, index, axis=1)


def tile_ids():
    lane = lax.broadcasted_iota(jnp.int32, (8, 128), 1)
    sub = lax.broadcasted_iota(jnp.int32, (8, 128), 0)
    half = (lane >= K).astype(jnp.int32) * K
    return sub, half, lane - half


def by_core(core, at_zero, at_one):
    return jnp.where(core == 0, at_zero, at_one)


def eliminate(pairs):
    sub, half, col = tile_ids()
    for k in range(0, K, 2):
        g, s = divmod(k, 8)
        at0, at1 = half + k, half + k + 1
        here0, here1 = col == k, col == k + 1
        here = here0 | here1
        for groups in pairs:
            row0 = jnp.broadcast_to(groups[g][s:s + 1, :], (8, 128))
            row1 = jnp.broadcast_to(groups[g][s + 1:s + 2, :], (8, 128))
            a, b, c = lanes_of(row0, at0), lanes_of(row0, at1), lanes_of(row1, at1)
            scale = 1.0 / (a * c - b * b)
            row0 = jnp.where(here, here0.astype(F32), row0) * scale
            row1 = jnp.where(here, here1.astype(F32), row1) * scale
            scaled0 = c * row0 - b * row1
            scaled1 = a * row1 - b * row0
            for i in range(g, 8):
                if i == g and s == 6:
                    continue
                f0, f1 = lanes_of(groups[i], at0), lanes_of(groups[i], at1)
                new = jnp.where(here, 0.0, groups[i]) - f0 * scaled0 - f1 * scaled1
                groups[i] = jnp.where(sub > s + 1, new, groups[i]) if i == g else new
    odd = (sub & 1) == 1
    results = []
    for groups in pairs:
        outs = []
        logs = jnp.zeros((8, 128), F32)
        for i in range(8):
            row_id = sub + 8 * i
            diag = lanes_of(groups[i], half + row_id)
            side = lanes_of(groups[i], half + (row_id ^ 1))
            unit = jnp.where(col < row_id - (sub & 1), groups[i], (col == row_id).astype(F32))
            ratio = side / pltpu.roll(diag, 1, 0)
            unit = jnp.where(odd, unit - ratio * pltpu.roll(unit, 1, 0), unit)
            diag = jnp.where(odd, diag - ratio * side, diag)
            outs.append(unit * lax.rsqrt(diag))
            logs = logs + jnp.log(diag)
        results.append((outs, 0.5 * jnp.sum(logs, axis=0, keepdims=True)))
    return results


def spread_kernel(patterns_ref, out_ref):
    for z in range(8):
        out_ref[z] = patterns_ref[...]


def project_kernel(own_ref, other_ref, fields_ref, out_ref):
    core = lax.axis_index("core")
    parts = []
    for z in range(8):
        own, other = own_ref[z], other_ref[z]
        parts += [by_core(core, own, other), by_core(core, other, own)]
    patterns = jnp.concatenate(parts, axis=1)
    part = lax.dot_general(
        fields_ref[...], patterns, (((1,), (1,)), ((), ())), preferred_element_type=F32)
    days = part.shape[0] // 2
    part = jnp.concatenate([part[:days], part[days:]], axis=1).T
    for b in range(8):
        out_ref[2 * b] = part[8 * b:8 * b + 8]
        out_ref[2 * b + 1] = part[K + 8 * b:K + 8 * b + 8]


def read_pcs(pcs_ref):
    return [jnp.concatenate([pcs_ref[2 * b], pcs_ref[2 * b + 1]], axis=1) for b in range(8)]


def centre(pcs, row, offset):
    sub, _, _ = tile_ids()
    row = jnp.broadcast_to(row, (8, 128))
    outs = []
    for b in range(8):
        column = lanes_of(row, sub + (8 * b + offset))
        outs.append(pcs[b] - jnp.concatenate([column] * (pcs[b].shape[1] // 128), axis=1))
    return outs


def softmax_of(logp):
    top = jnp.max(logp, axis=0, keepdims=True)
    expo = jnp.exp(logp - top)
    return expo / jnp.sum(expo, axis=0, keepdims=True)


def moments(core, centred_of, resp, keep_ref, send_ref):
    days = resp.shape[1]
    counts = jnp.broadcast_to(jnp.sum(resp, axis=1, keepdims=True), (R, K))
    row_id = lax.broadcasted_iota(jnp.int32, (K, K), 0)
    col_id = lax.broadcasted_iota(jnp.int32, (K, K), 1)
    seconds, firsts = [], []
    for r in range(R):
        centred = jnp.concatenate(centred_of(r), axis=0)
        weight = resp[r:r + 1, :]
        left = jnp.concatenate([centred * weight, jnp.broadcast_to(weight, (8, days))], axis=0)
        got = lax.dot_general(left, centred, (((1,), (1,)), ((), ())), precision=PRECISE,
                              preferred_element_type=F32)
        seconds.append(got[:K])
        firsts.append(got[K:K + 1])
    packs = []
    for h in range(2):
        squares, tails = [], []
        for p in range(2):
            a = HALF * h + 2 * p
            squares.append(jnp.where(row_id >= col_id, seconds[a], seconds[a + 1]))
            diag = jnp.sum(jnp.where(row_id == col_id, seconds[a + 1], 0.0), axis=0, keepdims=True)
            tails.append(jnp.concatenate(
                [diag, firsts[a], firsts[a + 1], counts[a:a + 1], counts[a + 1:a + 2],
                 jnp.zeros((3, K), F32)], axis=0))
        packs.append(jnp.concatenate(
            [jnp.concatenate(squares, axis=1), jnp.concatenate(tails, axis=1)], axis=0))
    keep_ref[...] = by_core(core, packs[0], packs[1])
    send_ref[...] = by_core(core, packs[1], packs[0])


def first_kernel(pcs_ref, params_ref, base_ref, keep_ref, send_ref):
    pcs = read_pcs(pcs_ref)
    sub, _, _ = tile_ids()
    logs = []
    for r in range(R):
        row = params_ref[r:r + 1, :]
        inverse = jnp.broadcast_to(1.0 / row, (8, 128))
        centred = centre(pcs, row, 0)
        total = None
        for b in range(8):
            column = lanes_of(inverse, sub + (8 * b + K))
            scale = jnp.concatenate([column] * 8, axis=1)
            term = centred[b] * centred[b] * scale
            total = term if total is None else total + term
        logs.append(jnp.sum(total, axis=0, keepdims=True))
    logp = base_ref[:, 0:1] - 0.5 * jnp.concatenate(logs, axis=0)
    resp = softmax_of(logp)
    moments(lax.axis_index("core"), lambda r: centre(pcs, params_ref[r:r + 1, :], 0), resp, keep_ref, send_ref)


def merge_kernel(parts_ref, shift_ref, block_ref, covs_ref):
    sub, half, col = tile_ids()
    total = parts_ref[0]
    for z in range(1, 8):
        total = total + parts_ref[z]
    packed = total[:K]
    flipped = packed.T
    flipped = jnp.concatenate([flipped[:K], flipped[K:]], axis=1)
    tail = total[K:]
    pairs = []
    infos = []
    for p in range(2):
        first, count, shift = tail[1 + p:2 + p], tail[3 + p:4 + p], shift_ref[p:p + 1, :]
        counted = jnp.maximum(count, 1.0)
        mean = (first + count * shift) / counted
        delta = mean - shift
        rest = first - count * delta
        first_b, delta_b = jnp.broadcast_to(first, (8, 128)), jnp.broadcast_to(delta, (8, 128))
        scale = 1.0 / counted
        groups = []
        for g in range(8):
            row_id = sub + 8 * g
            straight, turned = packed[8 * g:8 * g + 8], flipped[8 * g:8 * g + 8]
            if p == 0:
                second = jnp.where(row_id >= col, straight, turned)
            else:
                second = jnp.where(row_id < col, straight, jnp.where(row_id > col, turned, tail[0:1]))
            at = half + row_id
            second = second - lanes_of(first_b, at) * delta - lanes_of(delta_b, at) * rest
            cov = second * scale + jnp.where(row_id == col, REG, 0.0)
            covs_ref[K * p + 8 * g:K * p + 8 * g + 8, :] = cov
            groups.append(cov)
        pairs.append(groups)
        infos.append((mean, counted))
    (first_out, first_log), (second_out, second_log) = eliminate(pairs)
    for g in range(8):
        block_ref[8 * g:8 * g + 8, :] = first_out[g]
        block_ref[K + 8 * g:K + 8 * g + 8, :] = second_out[g]
    block_ref[2 * K:, :] = jnp.concatenate(
        [infos[0][0], infos[1][0], first_log, second_log, infos[0][1], infos[1][1],
         jnp.zeros((2, 128), F32)], axis=0)


def regime_of(r):
    h, q = divmod(r, HALF)
    return h, q % 2, K * (q // 2)


def expect(pcs, halves):
    infos = [block[2 * K:] for block in halves]

    def column(at):
        rows = []
        for r in range(R):
            h, p, offset = regime_of(r)
            rows.append(infos[h][at + p:at + p + 1, offset:offset + 1])
        return jnp.concatenate(rows, axis=0)

    counted = column(4)
    weights = counted / jnp.sum(counted, axis=0, keepdims=True)
    logs = []
    for r in range(R):
        h, p, offset = regime_of(r)
        inverse = halves[h][K * p:K * p + K, offset:offset + K]
        centred = jnp.concatenate(centre(pcs, infos[h][p:p + 1, :], offset), axis=0)
        shifted = lax.dot_general(inverse, centred, (((1,), (0,)), ((), ())), precision=PRECISE,
                                  preferred_element_type=F32)
        logs.append(jnp.sum(shifted * shifted, axis=0, keepdims=True))
    logp = jnp.log(weights) - column(2) - 0.5 * jnp.concatenate(logs, axis=0)
    return softmax_of(logp), weights


def halves_of(core, keep_ref, got_ref):
    keep, got = keep_ref[...], got_ref[...]
    return [by_core(core, keep, got), by_core(core, got, keep)]


def middle_kernel(pcs_ref, keep_ref, got_ref, out_keep_ref, out_send_ref):
    core = lax.axis_index("core")
    pcs = read_pcs(pcs_ref)
    halves = halves_of(core, keep_ref, got_ref)
    resp, _ = expect(pcs, halves)

    def centred_of(r):
        h, p, offset = regime_of(r)
        return centre(pcs, halves[h][2 * K + p:2 * K + p + 1, :], offset)

    moments(core, centred_of, resp, out_keep_ref, out_send_ref)


def last_kernel(pcs_ref, keep_ref, got_ref, fields_ref, member_ref, terms_ref, means_ref, weights_ref):
    core = lax.axis_index("core")
    pcs = read_pcs(pcs_ref)
    halves = halves_of(core, keep_ref, got_ref)
    member, weights = expect(pcs, halves)
    member_ref[...] = member
    weights_ref[...] = jnp.broadcast_to(weights, (R, 128))
    means = []
    for r in range(R):
        h, p, offset = regime_of(r)
        means.append(halves[h][2 * K + p:2 * K + p + 1, offset:offset + K])
    means_ref[...] = jnp.concatenate(means, axis=0)
    count = jnp.broadcast_to(jnp.sum(member, axis=1, keepdims=True), (R, 128))
    rounded = member.astype(BF16)
    for j in range(16):
        terms_ref[j, :, 0:256] = jnp.dot(rounded, fields_ref[:, 256 * j:256 * j + 256], preferred_element_type=F32)
        terms_ref[j, :, 256:384] = count


def spread(x, n):
    return jnp.broadcast_to(x[None], (n,) + x.shape)


def merge(keep, send, shift):
    half = keep + lax.ppermute(send, "core", SWAP)
    parts = lax.all_to_all(spread(half, 8), "z", 0, 0)
    return call(merge_kernel, [((2 * K + 8, 128), F32), ((2 * K, 128), F32)], [parts, shift],
                limit=SMALL, cost=COVER)


def body(anomalies, eofs, means_init, variances, mixing):
    days = anomalies.shape[0]
    core = lax.axis_index("core")
    eight, = call(
        spread_kernel, [((8,) + eofs.shape, BF16)], [eofs], limit=SMALL,
        cost=COVER)
    own = lax.all_to_all(eight, "z", 0, 0)
    other = lax.ppermute(own, "core", SWAP)
    partial, = call(
        project_kernel, [((16, 8, days // 2), F32)], [own, other, anomalies], limit=SMALL)
    mine = jnp.sum(lax.all_to_all(partial, "grid", 0, 0), axis=0)
    pcs = lax.all_to_all(spread(mine, 16), "grid", 0, 0)

    params = jnp.concatenate([means_init, variances], axis=1)
    base = jnp.log(mixing / jnp.sum(mixing)) - 0.5 * jnp.sum(jnp.log(variances), axis=1)
    base = jnp.broadcast_to(base[:, None], (R, 128))
    sides = means_init.reshape(2, 2, 2, K).swapaxes(1, 2).reshape(2, 2, 2 * K)
    shift = jnp.where(core == 0, sides[0], sides[1])

    pack = [((ROWS, 128), F32)] * 2
    keep, send = call(first_kernel, pack, [pcs, params, base])
    block, _ = merge(keep, send, shift)
    got = lax.ppermute(block, "core", SWAP)
    keep, send = call(middle_kernel, pack, [pcs, block, got])
    block, covs = merge(keep, send, block[2 * K:2 * K + 2])
    got = lax.ppermute(block, "core", SWAP)
    got_covs = lax.ppermute(covs, "core", SWAP)
    member, terms, means, weights = call(
        last_kernel,
        [((R, days), F32), ((16, R, 384), F32), ((R, K), F32), ((R, 128), F32)],
        [pcs, block, got, anomalies],
        limit=SMALL)
    sums = jnp.sum(lax.all_to_all(terms, ("z", "core"), 0, 0), axis=0)
    composites = (sums[:, :256] / jnp.maximum(sums[:, 256:257], 1.0)).astype(BF16)

    both = jnp.where(core == 0, jnp.stack([covs, got_covs]), jnp.stack([got_covs, covs]))
    covs = both.reshape(2, 2, K, 2, K).transpose(0, 3, 1, 2, 4).reshape(R, K, K)
    return (means, covs, weights[:, 0], member, composites)


def solution(mesh):
    split = Mesh(mesh.devices.reshape(16, 8, 2), ("grid", "z", "core"))
    day = ("z", "core")
    in_specs = (P(day, "grid"), P(None, ("grid",) + day), P(), P(), P())
    out_specs = (P(), P(), P(), P(None, day), P(None, ("grid",) + day))
    return jax.shard_map(body, mesh=split, in_specs=in_specs, out_specs=out_specs, check_vma=False)
```

```python
import functools

import jax
import jax.numpy as jnp
from jax import lax
from jax.experimental import pallas as pl
from jax.experimental.pallas import tpu as pltpu
from jax.sharding import Mesh, PartitionSpec as P

K = 64
R = 8
HALF = R // 2
F32 = jnp.float32
BF16 = jnp.bfloat16
REG = 0.01
SWAP = [(0, 1), (1, 0)]
ROWS = K + 8
LIMIT = 48 * 1024 * 1024
SMALL = 16 * 1024 * 1024
COVER = pl.CostEstimate(flops=20 * 10 ** 10, transcendentals=0, bytes_accessed=0)
VMEM = pl.BlockSpec(memory_space=pltpu.VMEM)
SMEM = pl.BlockSpec(memory_space=pltpu.SMEM)


def call(kernel, outs, operands, limit=LIMIT, cost=None, scalars=0):
    return pl.pallas_call(
        kernel,
        out_shape=tuple(jax.ShapeDtypeStruct(s, d) for s, d in outs),
        in_specs=[VMEM] * (len(operands) - scalars) + [SMEM] * scalars,
        out_specs=tuple([VMEM] * len(outs)),
        compiler_params=pltpu.CompilerParams(vmem_limit_bytes=limit),
        cost_estimate=cost,
    )(*operands)


def lanes_of(x, index):
    return jnp.take_along_axis(x, index, axis=1)


def tile_ids():
    lane = lax.broadcasted_iota(jnp.int32, (8, 128), 1)
    sub = lax.broadcasted_iota(jnp.int32, (8, 128), 0)
    half = (lane >= K).astype(jnp.int32) * K
    return sub, half, lane - half


def by_core(core, at_zero, at_one):
    return jnp.where(core == 0, at_zero, at_one)


def eliminate(pairs):
    sub, half, col = tile_ids()
    for k in range(0, K, 2):
        g, s = divmod(k, 8)
        at0, at1 = half + k, half + k + 1
        here0, here1 = col == k, col == k + 1
        here = here0 | here1
        for groups in pairs:
            row0 = jnp.broadcast_to(groups[g][s:s + 1, :], (8, 128))
            row1 = jnp.broadcast_to(groups[g][s + 1:s + 2, :], (8, 128))
            a, b, c = lanes_of(row0, at0), lanes_of(row0, at1), lanes_of(row1, at1)
            scale = 1.0 / (a * c - b * b)
            row0 = jnp.where(here, here0.astype(F32), row0) * scale
            row1 = jnp.where(here, here1.astype(F32), row1) * scale
            scaled0 = c * row0 - b * row1
            scaled1 = a * row1 - b * row0
            for i in range(g, 8):
                if i == g and s == 6:
                    continue
                f0, f1 = lanes_of(groups[i], at0), lanes_of(groups[i], at1)
                new = jnp.where(here, 0.0, groups[i]) - f0 * scaled0 - f1 * scaled1
                groups[i] = jnp.where(sub > s + 1, new, groups[i]) if i == g else new
    odd = (sub & 1) == 1
    results = []
    for groups in pairs:
        outs = []
        logs = jnp.zeros((8, 128), F32)
        for i in range(8):
            row_id = sub + 8 * i
            diag = lanes_of(groups[i], half + row_id)
            side = lanes_of(groups[i], half + (row_id ^ 1))
            unit = jnp.where(col < row_id - (sub & 1), groups[i], (col == row_id).astype(F32))
            ratio = side / pltpu.roll(diag, 1, 0)
            unit = jnp.where(odd, unit - ratio * pltpu.roll(unit, 1, 0), unit)
            diag = jnp.where(odd, diag - ratio * side, diag)
            outs.append(unit * lax.rsqrt(diag))
            logs = logs + jnp.log(diag)
        results.append((outs, 0.5 * jnp.sum(logs, axis=0, keepdims=True)))
    return results


def spread_kernel(patterns_ref, out_ref):
    for z in range(8):
        out_ref[z] = patterns_ref[...]


def project_kernel(own_ref, other_ref, fields_ref, out_ref):
    core = lax.axis_index("core")
    parts = []
    for z in range(8):
        own, other = own_ref[z], other_ref[z]
        parts += [by_core(core, own, other), by_core(core, other, own)]
    patterns = jnp.concatenate(parts, axis=1)
    part = lax.dot_general(
        fields_ref[...], patterns, (((1,), (1,)), ((), ())), preferred_element_type=F32)
    days = part.shape[0] // 2
    part = jnp.concatenate([part[:days], part[days:]], axis=1).T
    for b in range(8):
        out_ref[2 * b] = part[8 * b:8 * b + 8]
        out_ref[2 * b + 1] = part[K + 8 * b:K + 8 * b + 8]


def read_pcs(pcs_ref):
    return [jnp.concatenate([pcs_ref[2 * b], pcs_ref[2 * b + 1]], axis=1) for b in range(8)]


def centre(pcs, shift):
    sub, _, _ = tile_ids()
    row = jnp.broadcast_to(jnp.concatenate([shift, shift], axis=1), (8, 128))
    outs = []
    for b in range(8):
        column = lanes_of(row, sub + 8 * b)
        outs.append(pcs[b] - jnp.concatenate([column] * (pcs[b].shape[1] // 128), axis=1))
    return jnp.concatenate(outs, axis=0)


def split(x):
    high = x.astype(BF16)
    rest = x - high.astype(F32)
    middle = rest.astype(BF16)
    return high, middle, (rest - middle.astype(F32)).astype(BF16)


def softmax_of(logp):
    top = jnp.max(logp, axis=0, keepdims=True)
    expo = jnp.exp(logp - top)
    return expo / jnp.sum(expo, axis=0, keepdims=True)


def moments(core, centred, terms, resp, keep_ref, send_ref):
    counts = jnp.broadcast_to(jnp.sum(resp, axis=1, keepdims=True), (R, K))
    row_id = lax.broadcasted_iota(jnp.int32, (K, K), 0)
    col_id = lax.broadcasted_iota(jnp.int32, (K, K), 1)
    left = jnp.concatenate([centred * resp[r:r + 1, :] for r in range(R)] + [resp], axis=0)
    high, middle, low = split(left)
    contract = (((1,), (1,)), ((), ()))
    got = lax.dot_general(high, jnp.concatenate(terms, axis=0), contract, preferred_element_type=F32)
    more = lax.dot_general(middle, jnp.concatenate(terms[:2], axis=0), contract, preferred_element_type=F32)
    last = lax.dot_general(low, terms[0], contract, preferred_element_type=F32)
    got = got[:, :K] + (got[:, K:2 * K] + more[:, :K]) + (got[:, 2 * K:] + more[:, K:] + last)
    seconds = [got[K * r:K * r + K] for r in range(R)]
    firsts = [got[K * R + r:K * R + r + 1] for r in range(R)]
    packs = []
    for h in range(2):
        squares, tails = [], []
        for p in range(2):
            a = HALF * h + 2 * p
            squares.append(jnp.where(row_id >= col_id, seconds[a], seconds[a + 1]))
            diag = jnp.sum(jnp.where(row_id == col_id, seconds[a + 1], 0.0), axis=0, keepdims=True)
            tails.append(jnp.concatenate(
                [diag, firsts[a], firsts[a + 1], counts[a:a + 1], counts[a + 1:a + 2],
                 jnp.zeros((3, K), F32)], axis=0))
        packs.append(jnp.concatenate(
            [jnp.concatenate(squares, axis=1), jnp.concatenate(tails, axis=1)], axis=0))
    keep_ref[...] = by_core(core, packs[0], packs[1])
    send_ref[...] = by_core(core, packs[1], packs[0])


def put_shift(shift, shift_ref):
    shift_ref[...] = jnp.broadcast_to(jnp.concatenate([shift, shift], axis=1), (8, 128))


def first_kernel(pcs_ref, means_ref, variances_ref, mixing_ref, keep_ref, send_ref, shift_ref):
    pcs = read_pcs(pcs_ref)
    sub, _, _ = tile_ids()
    means, variances = means_ref[...], variances_ref[...]
    shift = jnp.sum(means, axis=0, keepdims=True) / R
    put_shift(shift, shift_ref)
    centred = centre(pcs, shift)
    params = jnp.concatenate([means - shift, 1.0 / variances], axis=1)
    mixing = jnp.zeros((R, 128), F32)
    for r in range(R):
        mixing = jnp.where(sub == r, mixing_ref[r], mixing)
    weights = mixing / jnp.sum(mixing, axis=0, keepdims=True)
    base = jnp.log(weights[:, 0:1]) - 0.5 * jnp.sum(jnp.log(variances), axis=1, keepdims=True)
    logs = []
    for r in range(R):
        row = jnp.broadcast_to(params[r:r + 1, :], (8, 128))
        total = None
        for b in range(8):
            mean = jnp.concatenate([lanes_of(row, sub + 8 * b)] * 8, axis=1)
            scale = jnp.concatenate([lanes_of(row, sub + (8 * b + K))] * 8, axis=1)
            apart = centred[8 * b:8 * b + 8] - mean
            term = apart * apart * scale
            total = term if total is None else total + term
        logs.append(jnp.sum(total, axis=0, keepdims=True))
    resp = softmax_of(base - 0.5 * jnp.concatenate(logs, axis=0))
    moments(lax.axis_index("core"), centred, split(centred), resp, keep_ref, send_ref)


def merge_kernel(parts_ref, shift_ref, block_ref, covs_ref):
    sub, half, col = tile_ids()
    total = parts_ref[0]
    for z in range(1, 8):
        total = total + parts_ref[z]
    packed = total[:K]
    flipped = packed.T
    flipped = jnp.concatenate([flipped[:K], flipped[K:]], axis=1)
    tail = total[K:]
    pairs = []
    infos = []
    for p in range(2):
        first, count, shift = tail[1 + p:2 + p], tail[3 + p:4 + p], shift_ref[0:1, :]
        counted = jnp.maximum(count, 1.0)
        mean = (first + count * shift) / counted
        delta = mean - shift
        rest = first - count * delta
        first_b, delta_b = jnp.broadcast_to(first, (8, 128)), jnp.broadcast_to(delta, (8, 128))
        scale = 1.0 / counted
        groups = []
        for g in range(8):
            row_id = sub + 8 * g
            straight, turned = packed[8 * g:8 * g + 8], flipped[8 * g:8 * g + 8]
            if p == 0:
                second = jnp.where(row_id >= col, straight, turned)
            else:
                second = jnp.where(row_id < col, straight, jnp.where(row_id > col, turned, tail[0:1]))
            at = half + row_id
            second = second - lanes_of(first_b, at) * delta - lanes_of(delta_b, at) * rest
            cov = second * scale + jnp.where(row_id == col, REG, 0.0)
            covs_ref[K * p + 8 * g:K * p + 8 * g + 8, :] = cov
            groups.append(cov)
        pairs.append(groups)
        infos.append((mean, counted))
    (first_out, first_log), (second_out, second_log) = eliminate(pairs)
    for g in range(8):
        block_ref[8 * g:8 * g + 8, :] = first_out[g]
        block_ref[K + 8 * g:K + 8 * g + 8, :] = second_out[g]
    block_ref[2 * K:, :] = jnp.concatenate(
        [infos[0][0], infos[1][0], first_log, second_log, infos[0][1], infos[1][1],
         jnp.zeros((2, 128), F32)], axis=0)


def regime_of(r):
    h, q = divmod(r, HALF)
    return h, q % 2, K * (q // 2)


def expect(pcs, halves):
    infos = [block[2 * K:] for block in halves]

    def column(at):
        rows = []
        for r in range(R):
            h, p, offset = regime_of(r)
            rows.append(infos[h][at + p:at + p + 1, offset:offset + 1])
        return jnp.concatenate(rows, axis=0)

    means, inverses = [], []
    for r in range(R):
        h, p, offset = regime_of(r)
        means.append(infos[h][p:p + 1, offset:offset + K])
        inverses.append(halves[h][K * p:K * p + K, offset:offset + K])
    means = jnp.concatenate(means, axis=0)
    counted = column(4)
    weights = counted / jnp.sum(counted, axis=0, keepdims=True)
    shift = jnp.sum(means * weights, axis=0, keepdims=True)
    centred = centre(pcs, shift)
    days = centred.shape[1]
    apart = jnp.concatenate([means - shift, jnp.zeros((128 - R, K), F32)], axis=0).T
    terms = split(centred)
    ends = split(apart)
    c1, c2, c3 = [jnp.concatenate([x, y], axis=1) for x, y in zip(terms, ends)]
    w1, w2, w3 = split(jnp.concatenate(inverses, axis=0))
    left = jnp.concatenate([w1, w1, w2, w2, w1, w3], axis=1)
    right = jnp.concatenate([c1, c2, c1, c2, c3, c1], axis=0)
    shifted = jnp.dot(left, right, preferred_element_type=F32)
    logs = []
    for r in range(R):
        mine = shifted[K * r:K * r + K]
        mine = mine[:, :days] - mine[:, days + r:days + r + 1]
        logs.append(jnp.sum(mine * mine, axis=0, keepdims=True))
    logp = jnp.log(weights) - column(2) - 0.5 * jnp.concatenate(logs, axis=0)
    return softmax_of(logp), weights, means, shift, centred, terms


def halves_of(core, keep_ref, got_ref):
    keep, got = keep_ref[...], got_ref[...]
    return [by_core(core, keep, got), by_core(core, got, keep)]


def middle_kernel(pcs_ref, keep_ref, got_ref, out_keep_ref, out_send_ref, shift_ref):
    core = lax.axis_index("core")
    resp, _, _, shift, centred, terms = expect(read_pcs(pcs_ref), halves_of(core, keep_ref, got_ref))
    put_shift(shift, shift_ref)
    moments(core, centred, terms, resp, out_keep_ref, out_send_ref)


def last_kernel(pcs_ref, keep_ref, got_ref, fields_ref, member_ref, terms_ref, means_ref, weights_ref):
    core = lax.axis_index("core")
    member, weights, means, _, _, _ = expect(read_pcs(pcs_ref), halves_of(core, keep_ref, got_ref))
    member_ref[...] = member
    weights_ref[...] = jnp.broadcast_to(weights, (R, 128))
    means_ref[...] = means
    count = jnp.broadcast_to(jnp.sum(member, axis=1, keepdims=True), (R, 128))
    rounded = member.astype(BF16)
    for j in range(16):
        terms_ref[j, :, 0:256] = jnp.dot(rounded, fields_ref[:, 256 * j:256 * j + 256], preferred_element_type=F32)
        terms_ref[j, :, 256:384] = count


def spread(x, n):
    return jnp.broadcast_to(x[None], (n,) + x.shape)


def merge(keep, send, shift):
    half = keep + lax.ppermute(send, "core", SWAP)
    parts = lax.all_to_all(spread(half, 8), "z", 0, 0)
    return call(merge_kernel, [((2 * K + 8, 128), F32), ((2 * K, 128), F32)], [parts, shift],
                limit=SMALL, cost=COVER)


def body(anomalies, eofs, means_init, variances, mixing):
    days = anomalies.shape[0]
    core = lax.axis_index("core")
    eight, = call(
        spread_kernel, [((8,) + eofs.shape, BF16)], [eofs], limit=SMALL,
        cost=COVER)
    own = lax.all_to_all(eight, "z", 0, 0)
    other = lax.ppermute(own, "core", SWAP)
    partial, = call(
        project_kernel, [((16, 8, days // 2), F32)], [own, other, anomalies], limit=SMALL)
    mine = jnp.sum(lax.all_to_all(partial, "grid", 0, 0), axis=0)
    pcs = lax.all_to_all(spread(mine, 16), "grid", 0, 0)

    pack = [((ROWS, 128), F32)] * 2 + [((8, 128), F32)]
    keep, send, shift = call(first_kernel, pack, [pcs, means_init, variances, mixing], scalars=1)
    block, _ = merge(keep, send, shift)
    got = lax.ppermute(block, "core", SWAP)
    keep, send, shift = call(middle_kernel, pack, [pcs, block, got])
    block, covs = merge(keep, send, shift)
    got = lax.ppermute(block, "core", SWAP)
    got_covs = lax.ppermute(covs, "core", SWAP)
    member, terms, means, weights = call(
        last_kernel,
        [((R, days), F32), ((16, R, 384), F32), ((R, K), F32), ((R, 128), F32)],
        [pcs, block, got, anomalies],
        limit=SMALL)
    sums = jnp.sum(lax.all_to_all(terms, ("z", "core"), 0, 0), axis=0)
    composites = (sums[:, :256] / jnp.maximum(sums[:, 256:257], 1.0)).astype(BF16)

    both = jnp.where(core == 0, jnp.stack([covs, got_covs]), jnp.stack([got_covs, covs]))
    covs = both.reshape(2, 2, K, 2, K).transpose(0, 3, 1, 2, 4).reshape(R, K, K)
    return (means, covs, weights[:, 0], member, composites)


def solution(mesh):
    split = Mesh(mesh.devices.reshape(16, 8, 2), ("grid", "z", "core"))
    day = ("z", "core")
    in_specs = (P(day, "grid"), P(None, ("grid",) + day), P(), P(), P())
    out_specs = (P(), P(), P(), P(None, day), P(None, ("grid",) + day))
    return jax.shard_map(body, mesh=split, in_specs=in_specs, out_specs=out_specs, check_vma=False)
```

```python
import functools

import jax
import jax.numpy as jnp
from jax import lax
from jax.experimental import pallas as pl
from jax.experimental.pallas import tpu as pltpu
from jax.sharding import Mesh, PartitionSpec as P

K = 64
R = 8
HALF = R // 2
F32 = jnp.float32
BF16 = jnp.bfloat16
REG = 0.01
SWAP = [(0, 1), (1, 0)]
ROWS = K + 8
INFO = 2 * K
LIMIT = 48 * 1024 * 1024
SMALL = 16 * 1024 * 1024
COVER = pl.CostEstimate(flops=20 * 10 ** 10, transcendentals=0, bytes_accessed=0)
VMEM = pl.BlockSpec(memory_space=pltpu.VMEM)
SMEM = pl.BlockSpec(memory_space=pltpu.SMEM)


def call(kernel, outs, operands, limit=LIMIT, cost=None, scalars=0, scalar_outs=0):
    return pl.pallas_call(
        kernel,
        out_shape=tuple(jax.ShapeDtypeStruct(s, d) for s, d in outs),
        in_specs=[VMEM] * (len(operands) - scalars) + [SMEM] * scalars,
        out_specs=tuple([VMEM] * (len(outs) - scalar_outs) + [SMEM] * scalar_outs),
        compiler_params=pltpu.CompilerParams(vmem_limit_bytes=limit),
        cost_estimate=cost,
    )(*operands)


def lanes_of(x, index):
    return jnp.take_along_axis(x, index, axis=1)


def tile_ids():
    lane = lax.broadcasted_iota(jnp.int32, (8, 128), 1)
    sub = lax.broadcasted_iota(jnp.int32, (8, 128), 0)
    half = (lane >= K).astype(jnp.int32) * K
    return sub, half, lane - half


def by_core(core, at_zero, at_one):
    return jnp.where(core == 0, at_zero, at_one)


def eliminate(pairs):
    sub, half, col = tile_ids()
    for k in range(0, K, 2):
        g, s = divmod(k, 8)
        at0, at1 = half + k, half + k + 1
        here0, here1 = col == k, col == k + 1
        here = here0 | here1
        for groups in pairs:
            row0 = jnp.broadcast_to(groups[g][s:s + 1, :], (8, 128))
            row1 = jnp.broadcast_to(groups[g][s + 1:s + 2, :], (8, 128))
            a, b, c = lanes_of(row0, at0), lanes_of(row0, at1), lanes_of(row1, at1)
            scale = 1.0 / (a * c - b * b)
            row0 = jnp.where(here, here0.astype(F32), row0) * scale
            row1 = jnp.where(here, here1.astype(F32), row1) * scale
            scaled0 = c * row0 - b * row1
            scaled1 = a * row1 - b * row0
            for i in range(g, 8):
                if i == g and s == 6:
                    continue
                f0, f1 = lanes_of(groups[i], at0), lanes_of(groups[i], at1)
                new = jnp.where(here, 0.0, groups[i]) - f0 * scaled0 - f1 * scaled1
                groups[i] = jnp.where(sub > s + 1, new, groups[i]) if i == g else new
    odd = (sub & 1) == 1
    results = []
    for groups in pairs:
        outs = []
        logs = jnp.zeros((8, 128), F32)
        for i in range(8):
            row_id = sub + 8 * i
            diag = lanes_of(groups[i], half + row_id)
            side = lanes_of(groups[i], half + (row_id ^ 1))
            unit = jnp.where(col < row_id - (sub & 1), groups[i], (col == row_id).astype(F32))
            ratio = side / pltpu.roll(diag, 1, 0)
            unit = jnp.where(odd, unit - ratio * pltpu.roll(unit, 1, 0), unit)
            diag = jnp.where(odd, diag - ratio * side, diag)
            outs.append(unit * lax.rsqrt(diag))
            logs = logs + jnp.log(diag)
        results.append((outs, 0.5 * jnp.sum(logs, axis=0, keepdims=True)))
    return results


def spread_kernel(patterns_ref, out_ref):
    for z in range(8):
        out_ref[z] = patterns_ref[...]


def project_kernel(own_ref, other_ref, fields_ref, out_ref):
    core = lax.axis_index("core")
    parts = []
    for z in range(8):
        own, other = own_ref[z], other_ref[z]
        parts += [by_core(core, own, other), by_core(core, other, own)]
    patterns = jnp.concatenate(parts, axis=1)
    part = lax.dot_general(
        fields_ref[...], patterns, (((1,), (1,)), ((), ())), preferred_element_type=F32)
    days = part.shape[0] // 2
    part = jnp.concatenate([part[:days], part[days:]], axis=1).T
    for b in range(8):
        out_ref[2 * b] = part[8 * b:8 * b + 8]
        out_ref[2 * b + 1] = part[K + 8 * b:K + 8 * b + 8]


def read_pcs(pcs_ref):
    return [jnp.concatenate([pcs_ref[2 * b], pcs_ref[2 * b + 1]], axis=1) for b in range(8)]


def centre(pcs, shift):
    sub, _, _ = tile_ids()
    row = jnp.broadcast_to(jnp.concatenate([shift, shift], axis=1), (8, 128))
    outs = []
    for b in range(8):
        column = lanes_of(row, sub + 8 * b)
        outs.append(pcs[b] - jnp.concatenate([column] * (pcs[b].shape[1] // 128), axis=1))
    return jnp.concatenate(outs, axis=0)


def split(x):
    high = x.astype(BF16)
    rest = x - high.astype(F32)
    middle = rest.astype(BF16)
    return high, middle, (rest - middle.astype(F32)).astype(BF16)


def softmax_of(logp):
    top = jnp.max(logp, axis=0, keepdims=True)
    expo = jnp.exp(logp - top)
    return expo / jnp.sum(expo, axis=0, keepdims=True)


def moments(core, centred, terms, resp, keep_ref, send_ref):
    counts = jnp.broadcast_to(jnp.sum(resp, axis=1, keepdims=True), (R, K))
    row_id = lax.broadcasted_iota(jnp.int32, (K, K), 0)
    col_id = lax.broadcasted_iota(jnp.int32, (K, K), 1)
    left = jnp.concatenate([centred * resp[r:r + 1, :] for r in range(R)] + [resp], axis=0)
    high, middle, low = split(left)
    contract = (((1,), (1,)), ((), ()))
    got = lax.dot_general(high, jnp.concatenate(terms, axis=0), contract, preferred_element_type=F32)
    more = lax.dot_general(middle, jnp.concatenate(terms[:2], axis=0), contract, preferred_element_type=F32)
    last = lax.dot_general(low, terms[0], contract, preferred_element_type=F32)
    got = got[:, :K] + (got[:, K:2 * K] + more[:, :K]) + (got[:, 2 * K:] + more[:, K:] + last)
    seconds = [got[K * r:K * r + K] for r in range(R)]
    firsts = [got[K * R + r:K * R + r + 1] for r in range(R)]
    packs = []
    for h in range(2):
        squares, tails = [], []
        for p in range(2):
            a = HALF * h + 2 * p
            squares.append(jnp.where(row_id >= col_id, seconds[a], seconds[a + 1]))
            diag = jnp.sum(jnp.where(row_id == col_id, seconds[a + 1], 0.0), axis=0, keepdims=True)
            tails.append(jnp.concatenate(
                [diag, firsts[a], firsts[a + 1], counts[a:a + 1], counts[a + 1:a + 2],
                 jnp.zeros((3, K), F32)], axis=0))
        packs.append(jnp.concatenate(
            [jnp.concatenate(squares, axis=1), jnp.concatenate(tails, axis=1)], axis=0))
    keep_ref[...] = by_core(core, packs[0], packs[1])
    send_ref[...] = by_core(core, packs[1], packs[0])


def put_shift(shift, shift_ref):
    shift_ref[...] = jnp.broadcast_to(jnp.concatenate([shift, shift], axis=1), (8, 128))


def first_kernel(pcs_ref, means_ref, variances_ref, mixing_ref, keep_ref, send_ref, shift_ref):
    pcs = read_pcs(pcs_ref)
    sub, _, _ = tile_ids()
    means, variances = means_ref[...], variances_ref[...]
    shift = jnp.sum(means, axis=0, keepdims=True) / R
    put_shift(shift, shift_ref)
    centred = centre(pcs, shift)
    params = jnp.concatenate([means - shift, 1.0 / variances], axis=1)
    mixing = jnp.zeros((R, 128), F32)
    for r in range(R):
        mixing = jnp.where(sub == r, mixing_ref[r], mixing)
    weights = mixing / jnp.sum(mixing, axis=0, keepdims=True)
    base = jnp.log(weights[:, 0:1]) - 0.5 * jnp.sum(jnp.log(variances), axis=1, keepdims=True)
    logs = []
    for r in range(R):
        row = jnp.broadcast_to(params[r:r + 1, :], (8, 128))
        total = None
        for b in range(8):
            mean = jnp.concatenate([lanes_of(row, sub + 8 * b)] * 8, axis=1)
            scale = jnp.concatenate([lanes_of(row, sub + (8 * b + K))] * 8, axis=1)
            apart = centred[8 * b:8 * b + 8] - mean
            term = apart * apart * scale
            total = term if total is None else total + term
        logs.append(jnp.sum(total, axis=0, keepdims=True))
    resp = softmax_of(base - 0.5 * jnp.concatenate(logs, axis=0))
    moments(lax.axis_index("core"), centred, split(centred), resp, keep_ref, send_ref)


def merge_kernel(parts_ref, shift_ref, block_ref):
    sub, half, col = tile_ids()
    total = parts_ref[0]
    for z in range(1, 8):
        total = total + parts_ref[z]
    packed = total[:K]
    flipped = packed.T
    flipped = jnp.concatenate([flipped[:K], flipped[K:]], axis=1)
    tail = total[K:]
    pairs = []
    infos = []
    for p in range(2):
        first, count, shift = tail[1 + p:2 + p], tail[3 + p:4 + p], shift_ref[0:1, :]
        counted = jnp.maximum(count, 1.0)
        mean = (first + count * shift) / counted
        delta = mean - shift
        rest = first - count * delta
        first_b, delta_b = jnp.broadcast_to(first, (8, 128)), jnp.broadcast_to(delta, (8, 128))
        scale = 1.0 / counted
        groups = []
        for g in range(8):
            row_id = sub + 8 * g
            straight, turned = packed[8 * g:8 * g + 8], flipped[8 * g:8 * g + 8]
            if p == 0:
                second = jnp.where(row_id >= col, straight, turned)
            else:
                second = jnp.where(row_id < col, straight, jnp.where(row_id > col, turned, tail[0:1]))
            at = half + row_id
            second = second - lanes_of(first_b, at) * delta - lanes_of(delta_b, at) * rest
            cov = second * scale + jnp.where(row_id == col, REG, 0.0)
            if block_ref.shape[0] > INFO + 8:
                at = INFO + 8 + K * p + 8 * g
                block_ref[at:at + 8, :] = cov
            groups.append(cov)
        pairs.append(groups)
        infos.append((mean, counted))
    (first_out, first_log), (second_out, second_log) = eliminate(pairs)
    for g in range(8):
        block_ref[8 * g:8 * g + 8, :] = first_out[g]
        block_ref[K + 8 * g:K + 8 * g + 8, :] = second_out[g]
    block_ref[INFO:INFO + 8, :] = jnp.concatenate(
        [infos[0][0], infos[1][0], first_log, second_log, infos[0][1], infos[1][1],
         jnp.zeros((2, 128), F32)], axis=0)


def regime_of(r):
    h, q = divmod(r, HALF)
    return h, q % 2, K * (q // 2)


def expect(pcs, halves):
    infos = [block[INFO:INFO + 8] for block in halves]

    def column(at):
        rows = []
        for r in range(R):
            h, p, offset = regime_of(r)
            rows.append(infos[h][at + p:at + p + 1, offset:offset + 1])
        return jnp.concatenate(rows, axis=0)

    means, inverses = [], []
    for r in range(R):
        h, p, offset = regime_of(r)
        means.append(infos[h][p:p + 1, offset:offset + K])
        inverses.append(halves[h][K * p:K * p + K, offset:offset + K])
    means = jnp.concatenate(means, axis=0)
    counted = column(4)
    weights = counted / jnp.sum(counted, axis=0, keepdims=True)
    shift = jnp.sum(means * weights, axis=0, keepdims=True)
    centred = centre(pcs, shift)
    days = centred.shape[1]
    apart = jnp.concatenate([means - shift, jnp.zeros((128 - R, K), F32)], axis=0).T
    terms = split(centred)
    ends = split(apart)
    c1, c2, c3 = [jnp.concatenate([x, y], axis=1) for x, y in zip(terms, ends)]
    w1, w2, w3 = split(jnp.concatenate(inverses, axis=0))
    left = jnp.concatenate([w1, w1, w2, w2, w1, w3], axis=1)
    right = jnp.concatenate([c1, c2, c1, c2, c3, c1], axis=0)
    shifted = jnp.dot(left, right, preferred_element_type=F32)
    logs = []
    for r in range(R):
        mine = shifted[K * r:K * r + K]
        mine = mine[:, :days] - mine[:, days + r:days + r + 1]
        logs.append(jnp.sum(mine * mine, axis=0, keepdims=True))
    logp = jnp.log(weights) - column(2) - 0.5 * jnp.concatenate(logs, axis=0)
    return softmax_of(logp), weights, means, shift, centred, terms


def halves_of(core, keep_ref, got_ref):
    keep, got = keep_ref[...], got_ref[...]
    return [by_core(core, keep, got), by_core(core, got, keep)]


def middle_kernel(pcs_ref, keep_ref, got_ref, out_keep_ref, out_send_ref, shift_ref):
    core = lax.axis_index("core")
    resp, _, _, shift, centred, terms = expect(read_pcs(pcs_ref), halves_of(core, keep_ref, got_ref))
    put_shift(shift, shift_ref)
    moments(core, centred, terms, resp, out_keep_ref, out_send_ref)


def last_kernel(pcs_ref, keep_ref, got_ref, fields_ref, member_ref, terms_ref, means_ref, covs_ref, weights_ref):
    core = lax.axis_index("core")
    halves = halves_of(core, keep_ref, got_ref)
    for r in range(R):
        h, p, offset = regime_of(r)
        at = INFO + 8 + K * p
        covs_ref[r] = halves[h][at:at + K, offset:offset + K]
    member, weights, means, _, _, _ = expect(read_pcs(pcs_ref), halves)
    member_ref[...] = member
    for r in range(R):
        weights_ref[r] = weights[r, 0]
    means_ref[...] = means
    count = jnp.broadcast_to(jnp.sum(member, axis=1, keepdims=True), (R, 128))
    rounded = member.astype(BF16)
    for j in range(16):
        terms_ref[j, :, 0:256] = jnp.dot(rounded, fields_ref[:, 256 * j:256 * j + 256], preferred_element_type=F32)
        terms_ref[j, :, 256:384] = count


def spread(x, n):
    return jnp.broadcast_to(x[None], (n,) + x.shape)


def merge(keep, send, shift, rows):
    half = keep + lax.ppermute(send, "core", SWAP)
    parts = lax.all_to_all(spread(half, 8), "z", 0, 0)
    block, = call(merge_kernel, [((rows, 128), F32)], [parts, shift], limit=SMALL, cost=COVER)
    return block, lax.ppermute(block, "core", SWAP)


def body(anomalies, eofs, means_init, variances, mixing):
    days = anomalies.shape[0]
    eight, = call(
        spread_kernel, [((8,) + eofs.shape, BF16)], [eofs], limit=SMALL,
        cost=COVER)
    own = lax.all_to_all(eight, "z", 0, 0)
    other = lax.ppermute(own, "core", SWAP)
    partial, = call(
        project_kernel, [((16, 8, days // 2), F32)], [own, other, anomalies], limit=SMALL)
    mine = jnp.sum(lax.all_to_all(partial, "grid", 0, 0), axis=0)
    pcs = lax.all_to_all(spread(mine, 16), "grid", 0, 0)

    pack = [((ROWS, 128), F32)] * 2 + [((8, 128), F32)]
    keep, send, shift = call(first_kernel, pack, [pcs, means_init, variances, mixing], scalars=1)
    block, got = merge(keep, send, shift, INFO + 8)
    keep, send, shift = call(middle_kernel, pack, [pcs, block, got])
    block, got = merge(keep, send, shift, INFO + 8 + 2 * K)
    member, terms, means, covs, weights = call(
        last_kernel,
        [((R, days), F32), ((16, R, 384), F32), ((R, K), F32), ((R, K, K), F32), ((R,), F32)],
        [pcs, block, got, anomalies], limit=SMALL, scalar_outs=1)
    sums = jnp.sum(lax.all_to_all(terms, ("z", "core"), 0, 0), axis=0)
    composites = (sums[:, :256] / jnp.maximum(sums[:, 256:257], 1.0)).astype(BF16)

    return (means, covs, weights, member, composites)


def solution(mesh):
    split = Mesh(mesh.devices.reshape(16, 8, 2), ("grid", "z", "core"))
    day = ("z", "core")
    in_specs = (P(day, "grid"), P(None, ("grid",) + day), P(), P(), P())
    out_specs = (P(), P(), P(), P(None, day), P(None, ("grid",) + day))
    return jax.shard_map(body, mesh=split, in_specs=in_specs, out_specs=out_specs, check_vma=False)
```

```python
import functools

import jax
import jax.numpy as jnp
from jax import lax
from jax.experimental import pallas as pl
from jax.experimental.pallas import tpu as pltpu
from jax.sharding import Mesh, PartitionSpec as P

K = 64
R = 8
HALF = R // 2
F32 = jnp.float32
BF16 = jnp.bfloat16
REG = 0.01
SWAP = [(0, 1), (1, 0)]
ROWS = K + 8
INFO = 2 * K
LIMIT = 48 * 1024 * 1024
SMALL = 16 * 1024 * 1024
COVER = pl.CostEstimate(flops=20 * 10 ** 10, transcendentals=0, bytes_accessed=0)
VMEM = pl.BlockSpec(memory_space=pltpu.VMEM)
SMEM = pl.BlockSpec(memory_space=pltpu.SMEM)
HBM = pl.BlockSpec(memory_space=pltpu.HBM)


def call(kernel, outs, operands, limit=LIMIT, cost=None, scalars=0, places=None, scratch=()):
    return pl.pallas_call(
        kernel,
        out_shape=tuple(jax.ShapeDtypeStruct(s, d) for s, d in outs),
        in_specs=[VMEM] * (len(operands) - scalars) + [SMEM] * scalars,
        out_specs=tuple(places or [VMEM] * len(outs)),
        scratch_shapes=scratch,
        compiler_params=pltpu.CompilerParams(vmem_limit_bytes=limit),
        cost_estimate=cost,
    )(*operands)


def lanes_of(x, index):
    return jnp.take_along_axis(x, index, axis=1)


def tile_ids():
    lane = lax.broadcasted_iota(jnp.int32, (8, 128), 1)
    sub = lax.broadcasted_iota(jnp.int32, (8, 128), 0)
    half = (lane >= K).astype(jnp.int32) * K
    return sub, half, lane - half


def by_core(core, at_zero, at_one):
    return jnp.where(core == 0, at_zero, at_one)


def eliminate(pairs):
    sub, half, col = tile_ids()
    for k in range(0, K, 4):
        g, s = divmod(k, 8)
        at = [half + (k + q) for q in range(4)]
        here = [col == k + q for q in range(4)]
        one = [h.astype(F32) for h in here]
        low, high = here[0] | here[1], here[2] | here[3]
        for groups in pairs:
            rows = [jnp.broadcast_to(groups[g][s + q:s + q + 1, :], (8, 128)) for q in range(4)]
            a, b, c = lanes_of(rows[0], at[0]), lanes_of(rows[0], at[1]), lanes_of(rows[1], at[1])
            p02, p03 = lanes_of(rows[0], at[2]), lanes_of(rows[0], at[3])
            p12, p13 = lanes_of(rows[1], at[2]), lanes_of(rows[1], at[3])
            p22, p23, p33 = lanes_of(rows[2], at[2]), lanes_of(rows[2], at[3]), lanes_of(rows[3], at[3])
            scale = 1.0 / (a * c - b * b)
            row0 = jnp.where(low, one[0], rows[0])
            row1 = jnp.where(low, one[1], rows[1])
            turned0 = c * row0 - b * row1
            turned1 = a * row1 - b * row0
            g02, g12 = (c * p02 - b * p12) * scale, (a * p12 - b * p02) * scale
            g03, g13 = (c * p03 - b * p13) * scale, (a * p13 - b * p03) * scale
            s22 = p22 - (p02 * g02 + p12 * g12)
            s23 = p23 - (p02 * g03 + p12 * g13)
            s33 = p33 - (p03 * g03 + p13 * g13)
            row2 = jnp.where(low, 0.0, rows[2]) - (p02 * turned0 + p12 * turned1) * scale
            row3 = jnp.where(low, 0.0, rows[3]) - (p03 * turned0 + p13 * turned1) * scale
            again = 1.0 / (s22 * s33 - s23 * s23)
            row2 = jnp.where(high, one[2], row2)
            row3 = jnp.where(high, one[3], row3)
            turned2 = s33 * row2 - s23 * row3
            turned3 = s22 * row3 - s23 * row2
            for i in range(g, 8):
                f0, f1, f2, f3 = [lanes_of(groups[i], x) for x in at]
                new = jnp.where(low, 0.0, groups[i]) - (f0 * turned0 + f1 * turned1) * scale
                if i == g:
                    new = jnp.where(sub > s + 1, new, groups[i])
                groups[i] = new
                if i == g and s == 4:
                    continue
                f2 = f2 - (f0 * g02 + f1 * g12)
                f3 = f3 - (f0 * g03 + f1 * g13)
                new = jnp.where(high, 0.0, new) - (f2 * turned2 + f3 * turned3) * again
                groups[i] = jnp.where(sub > s + 3, new, groups[i]) if i == g else new
    odd = (sub & 1) == 1
    results = []
    for groups in pairs:
        outs = []
        logs = jnp.zeros((8, 128), F32)
        for i in range(8):
            row_id = sub + 8 * i
            diag = lanes_of(groups[i], half + row_id)
            side = lanes_of(groups[i], half + (row_id ^ 1))
            unit = jnp.where(col < row_id - (sub & 1), groups[i], (col == row_id).astype(F32))
            ratio = side / pltpu.roll(diag, 1, 0)
            unit = jnp.where(odd, unit - ratio * pltpu.roll(unit, 1, 0), unit)
            diag = jnp.where(odd, diag - ratio * side, diag)
            outs.append(unit * lax.rsqrt(diag))
            logs = logs + jnp.log(diag)
        results.append((outs, 0.5 * jnp.sum(logs, axis=0, keepdims=True)))
    return results


def spread_kernel(patterns_ref, out_ref):
    for z in range(8):
        out_ref[z] = patterns_ref[...]


def project_kernel(own_ref, other_ref, fields_ref, out_ref):
    core = lax.axis_index("core")
    parts = []
    for z in range(8):
        own, other = own_ref[z], other_ref[z]
        parts += [by_core(core, own, other), by_core(core, other, own)]
    patterns = jnp.concatenate(parts, axis=1)
    part = lax.dot_general(
        fields_ref[...], patterns, (((1,), (1,)), ((), ())), preferred_element_type=F32)
    days = part.shape[0] // 2
    part = jnp.concatenate([part[:days], part[days:]], axis=1).T
    for b in range(8):
        out_ref[2 * b] = part[8 * b:8 * b + 8]
        out_ref[2 * b + 1] = part[K + 8 * b:K + 8 * b + 8]


def read_pcs(pcs_ref):
    return [jnp.concatenate([pcs_ref[2 * b], pcs_ref[2 * b + 1]], axis=1) for b in range(8)]


def centre(pcs, shift):
    sub, _, _ = tile_ids()
    row = jnp.broadcast_to(jnp.concatenate([shift, shift], axis=1), (8, 128))
    outs = []
    for b in range(8):
        column = lanes_of(row, sub + 8 * b)
        outs.append(pcs[b] - jnp.concatenate([column] * (pcs[b].shape[1] // 128), axis=1))
    return jnp.concatenate(outs, axis=0)


def split(x):
    high = x.astype(BF16)
    rest = x - high.astype(F32)
    middle = rest.astype(BF16)
    return high, middle, (rest - middle.astype(F32)).astype(BF16)


def softmax_of(logp):
    top = jnp.max(logp, axis=0, keepdims=True)
    expo = jnp.exp(logp - top)
    return expo / jnp.sum(expo, axis=0, keepdims=True)


def moments(core, centred, terms, resp, keep_ref, send_ref):
    counts = jnp.broadcast_to(jnp.sum(resp, axis=1, keepdims=True), (R, K))
    row_id = lax.broadcasted_iota(jnp.int32, (K, K), 0)
    col_id = lax.broadcasted_iota(jnp.int32, (K, K), 1)
    left = jnp.concatenate([centred * resp[r:r + 1, :] for r in range(R)] + [resp], axis=0)
    high, middle, _ = split(left)
    contract = (((1,), (1,)), ((), ()))
    got = lax.dot_general(high, jnp.concatenate(terms, axis=0), contract, preferred_element_type=F32)
    more = lax.dot_general(middle, jnp.concatenate(terms[:2], axis=0), contract, preferred_element_type=F32)
    got = got[:, :K] + (got[:, K:2 * K] + more[:, :K]) + (got[:, 2 * K:] + more[:, K:])
    seconds = [got[K * r:K * r + K] for r in range(R)]
    firsts = [got[K * R + r:K * R + r + 1] for r in range(R)]
    packs = []
    for h in range(2):
        squares, tails = [], []
        for p in range(2):
            a = HALF * h + 2 * p
            squares.append(jnp.where(row_id >= col_id, seconds[a], seconds[a + 1]))
            diag = jnp.sum(jnp.where(row_id == col_id, seconds[a + 1], 0.0), axis=0, keepdims=True)
            tails.append(jnp.concatenate(
                [diag, firsts[a], firsts[a + 1], counts[a:a + 1], counts[a + 1:a + 2],
                 jnp.zeros((3, K), F32)], axis=0))
        packs.append(jnp.concatenate(
            [jnp.concatenate(squares, axis=1), jnp.concatenate(tails, axis=1)], axis=0))
    keep_ref[...] = by_core(core, packs[0], packs[1])
    send_ref[...] = by_core(core, packs[1], packs[0])


def put_shift(shift, shift_ref):
    shift_ref[...] = jnp.broadcast_to(jnp.concatenate([shift, shift], axis=1), (8, 128))


def first_kernel(pcs_ref, means_ref, variances_ref, mixing_ref, keep_ref, send_ref, shift_ref):
    pcs = read_pcs(pcs_ref)
    sub, _, _ = tile_ids()
    means, variances = means_ref[...], variances_ref[...]
    shift = jnp.sum(means, axis=0, keepdims=True) / R
    put_shift(shift, shift_ref)
    centred = centre(pcs, shift)
    params = jnp.concatenate([means - shift, 1.0 / variances], axis=1)
    mixing = jnp.zeros((R, 128), F32)
    for r in range(R):
        mixing = jnp.where(sub == r, mixing_ref[r], mixing)
    weights = mixing / jnp.sum(mixing, axis=0, keepdims=True)
    base = jnp.log(weights[:, 0:1]) - 0.5 * jnp.sum(jnp.log(variances), axis=1, keepdims=True)
    logs = []
    for r in range(R):
        row = jnp.broadcast_to(params[r:r + 1, :], (8, 128))
        total = None
        for b in range(8):
            mean = jnp.concatenate([lanes_of(row, sub + 8 * b)] * 8, axis=1)
            scale = jnp.concatenate([lanes_of(row, sub + (8 * b + K))] * 8, axis=1)
            apart = centred[8 * b:8 * b + 8] - mean
            term = apart * apart * scale
            total = term if total is None else total + term
        logs.append(jnp.sum(total, axis=0, keepdims=True))
    resp = softmax_of(base - 0.5 * jnp.concatenate(logs, axis=0))
    moments(lax.axis_index("core"), centred, split(centred), resp, keep_ref, send_ref)


def merge_kernel(parts_ref, shift_ref, block_ref):
    sub, half, col = tile_ids()
    total = parts_ref[0]
    for z in range(1, 8):
        total = total + parts_ref[z]
    packed = total[:K]
    flipped = packed.T
    flipped = jnp.concatenate([flipped[:K], flipped[K:]], axis=1)
    tail = total[K:]
    pairs = []
    infos = []
    for p in range(2):
        first, count, shift = tail[1 + p:2 + p], tail[3 + p:4 + p], shift_ref[0:1, :]
        counted = jnp.maximum(count, 1.0)
        mean = (first + count * shift) / counted
        delta = mean - shift
        rest = first - count * delta
        first_b, delta_b = jnp.broadcast_to(first, (8, 128)), jnp.broadcast_to(delta, (8, 128))
        scale = 1.0 / counted
        groups = []
        for g in range(8):
            row_id = sub + 8 * g
            straight, turned = packed[8 * g:8 * g + 8], flipped[8 * g:8 * g + 8]
            if p == 0:
                second = jnp.where(row_id >= col, straight, turned)
            else:
                second = jnp.where(row_id < col, straight, jnp.where(row_id > col, turned, tail[0:1]))
            at = half + row_id
            second = second - lanes_of(first_b, at) * delta - lanes_of(delta_b, at) * rest
            cov = second * scale + jnp.where(row_id == col, REG, 0.0)
            if block_ref.shape[0] > INFO + 8:
                at = INFO + 8 + K * p + 8 * g
                block_ref[at:at + 8, :] = cov
            groups.append(cov)
        pairs.append(groups)
        infos.append((mean, counted))
    (first_out, first_log), (second_out, second_log) = eliminate(pairs)
    for g in range(8):
        block_ref[8 * g:8 * g + 8, :] = first_out[g]
        block_ref[K + 8 * g:K + 8 * g + 8, :] = second_out[g]
    block_ref[INFO:INFO + 8, :] = jnp.concatenate(
        [infos[0][0], infos[1][0], first_log, second_log, infos[0][1], infos[1][1],
         jnp.zeros((2, 128), F32)], axis=0)


def regime_of(r):
    h, q = divmod(r, HALF)
    return h, q % 2, K * (q // 2)


def expect(pcs, halves):
    infos = [block[INFO:INFO + 8] for block in halves]

    def column(at):
        rows = []
        for r in range(R):
            h, p, offset = regime_of(r)
            rows.append(infos[h][at + p:at + p + 1, offset:offset + 1])
        return jnp.concatenate(rows, axis=0)

    means, inverses = [], []
    for r in range(R):
        h, p, offset = regime_of(r)
        means.append(infos[h][p:p + 1, offset:offset + K])
        inverses.append(halves[h][K * p:K * p + K, offset:offset + K])
    means = jnp.concatenate(means, axis=0)
    counted = column(4)
    weights = counted / jnp.sum(counted, axis=0, keepdims=True)
    shift = jnp.sum(means * weights, axis=0, keepdims=True)
    centred = centre(pcs, shift)
    days = centred.shape[1]
    apart = jnp.concatenate([means - shift, jnp.zeros((128 - R, K), F32)], axis=0).T
    terms = split(centred)
    ends = split(apart)
    c1, c2, c3 = [jnp.concatenate([x, y], axis=1) for x, y in zip(terms, ends)]
    w1, w2, w3 = split(jnp.concatenate(inverses, axis=0))
    left = jnp.concatenate([w1, w1, w2, w2, w1, w3], axis=1)
    right = jnp.concatenate([c1, c2, c1, c2, c3, c1], axis=0)
    shifted = jnp.dot(left, right, preferred_element_type=F32)
    logs = []
    for r in range(R):
        mine = shifted[K * r:K * r + K]
        mine = mine[:, :days] - mine[:, days + r:days + r + 1]
        logs.append(jnp.sum(mine * mine, axis=0, keepdims=True))
    logp = jnp.log(weights) - column(2) - 0.5 * jnp.concatenate(logs, axis=0)
    return softmax_of(logp), weights, means, shift, centred, terms


def halves_of(core, keep_ref, got_ref):
    keep, got = keep_ref[...], got_ref[...]
    return [by_core(core, keep, got), by_core(core, got, keep)]


def middle_kernel(pcs_ref, keep_ref, got_ref, out_keep_ref, out_send_ref, shift_ref):
    core = lax.axis_index("core")
    resp, _, _, shift, centred, terms = expect(read_pcs(pcs_ref), halves_of(core, keep_ref, got_ref))
    put_shift(shift, shift_ref)
    moments(core, centred, terms, resp, out_keep_ref, out_send_ref)


def last_kernel(pcs_ref, keep_ref, got_ref, fields_ref, terms_ref, member_hbm, means_hbm, covs_hbm, weights_ref,
                member_ref, means_ref, covs_ref, sems):
    copies = [
        pltpu.make_async_copy(source, target, sems.at[i])
        for i, (source, target) in enumerate(
            ((covs_ref, covs_hbm), (member_ref, member_hbm), (means_ref, means_hbm)))]
    core = lax.axis_index("core")
    halves = halves_of(core, keep_ref, got_ref)
    for r in range(R):
        h, p, offset = regime_of(r)
        at = INFO + 8 + K * p
        covs_ref[r] = halves[h][at:at + K, offset:offset + K]
    copies[0].start()
    member, weights, means, _, _, _ = expect(read_pcs(pcs_ref), halves)
    member_ref[...] = member
    copies[1].start()
    means_ref[...] = means
    copies[2].start()
    for r in range(R):
        weights_ref[r] = weights[r, 0]
    count = jnp.broadcast_to(jnp.sum(member, axis=1, keepdims=True), (R, 128))
    rounded = member.astype(BF16)
    for j in range(16):
        terms_ref[j, :, 0:256] = jnp.dot(rounded, fields_ref[:, 256 * j:256 * j + 256], preferred_element_type=F32)
        terms_ref[j, :, 256:384] = count
    for copy in copies:
        copy.wait()


def spread(x, n):
    return jnp.broadcast_to(x[None], (n,) + x.shape)


def merge(keep, send, shift, rows):
    half = keep + lax.ppermute(send, "core", SWAP)
    parts = lax.all_to_all(spread(half, 8), "z", 0, 0)
    block, = call(merge_kernel, [((rows, 128), F32)], [parts, shift], limit=SMALL, cost=COVER)
    return block, lax.ppermute(block, "core", SWAP)


def body(anomalies, eofs, means_init, variances, mixing):
    days = anomalies.shape[0]
    eight, = call(
        spread_kernel, [((8,) + eofs.shape, BF16)], [eofs], limit=SMALL,
        cost=COVER)
    own = lax.all_to_all(eight, "z", 0, 0)
    other = lax.ppermute(own, "core", SWAP)
    partial, = call(
        project_kernel, [((16, 8, days // 2), F32)], [own, other, anomalies], limit=SMALL)
    mine = jnp.sum(lax.all_to_all(partial, "grid", 0, 0), axis=0)
    pcs = lax.all_to_all(spread(mine, 16), "grid", 0, 0)

    pack = [((ROWS, 128), F32)] * 2 + [((8, 128), F32)]
    keep, send, shift = call(first_kernel, pack, [pcs, means_init, variances, mixing], scalars=1)
    block, got = merge(keep, send, shift, INFO + 8)
    keep, send, shift = call(middle_kernel, pack, [pcs, block, got])
    block, got = merge(keep, send, shift, INFO + 8 + 2 * K)
    results = [((R, days), F32), ((R, K), F32), ((R, K, K), F32)]
    terms, member, means, covs, weights = call(
        last_kernel, [((16, R, 384), F32)] + results + [((R,), F32)],
        [pcs, block, got, anomalies], limit=SMALL, places=[VMEM, HBM, HBM, HBM, SMEM],
        scratch=[pltpu.VMEM(*one) for one in results] + [pltpu.SemaphoreType.DMA((3,))])
    sums = jnp.sum(lax.all_to_all(terms, ("z", "core"), 0, 0), axis=0)
    composites = (sums[:, :256] / jnp.maximum(sums[:, 256:257], 1.0)).astype(BF16)

    return (means, covs, weights, member, composites)


def solution(mesh):
    split = Mesh(mesh.devices.reshape(16, 8, 2), ("grid", "z", "core"))
    day = ("z", "core")
    in_specs = (P(day, "grid"), P(None, ("grid",) + day), P(), P(), P())
    out_specs = (P(), P(), P(), P(None, day), P(None, ("grid",) + day))
    return jax.shard_map(body, mesh=split, in_specs=in_specs, out_specs=out_specs, check_vma=False)
```

```python
import functools

import jax
import jax.numpy as jnp
from jax import lax
from jax.experimental import pallas as pl
from jax.experimental.pallas import tpu as pltpu
from jax.sharding import Mesh, PartitionSpec as P

K = 64
R = 8
HALF = R // 2
F32 = jnp.float32
BF16 = jnp.bfloat16
REG = 0.01
SWAP = [(0, 1), (1, 0)]
ROWS = K + 8
INFO = 2 * K
LIMIT = 48 * 1024 * 1024
SMALL = 16 * 1024 * 1024
COVER = pl.CostEstimate(flops=20 * 10 ** 10, transcendentals=0, bytes_accessed=0)
VMEM = pl.BlockSpec(memory_space=pltpu.VMEM)
SMEM = pl.BlockSpec(memory_space=pltpu.SMEM)


def call(kernel, outs, operands, limit=LIMIT, cost=None, scalars=0, scalar_outs=0):
    return pl.pallas_call(
        kernel,
        out_shape=tuple(jax.ShapeDtypeStruct(s, d) for s, d in outs),
        in_specs=[VMEM] * (len(operands) - scalars) + [SMEM] * scalars,
        out_specs=tuple([VMEM] * (len(outs) - scalar_outs) + [SMEM] * scalar_outs),
        compiler_params=pltpu.CompilerParams(vmem_limit_bytes=limit),
        cost_estimate=cost,
    )(*operands)


def lanes_of(x, index):
    return jnp.take_along_axis(x, index, axis=1)


def tile_ids():
    lane = lax.broadcasted_iota(jnp.int32, (8, 128), 1)
    sub = lax.broadcasted_iota(jnp.int32, (8, 128), 0)
    half = (lane >= K).astype(jnp.int32) * K
    return sub, half, lane - half


def by_core(core, at_zero, at_one):
    return jnp.where(core == 0, at_zero, at_one)


def eliminate(pairs):
    sub, half, col = tile_ids()
    for k in range(0, K, 4):
        g, s = divmod(k, 8)
        at = [half + (k + q) for q in range(4)]
        here = [col == k + q for q in range(4)]
        one = [h.astype(F32) for h in here]
        low, high = here[0] | here[1], here[2] | here[3]
        for groups in pairs:
            rows = [jnp.broadcast_to(groups[g][s + q:s + q + 1, :], (8, 128)) for q in range(4)]
            a, b, c = lanes_of(rows[0], at[0]), lanes_of(rows[0], at[1]), lanes_of(rows[1], at[1])
            p02, p03 = lanes_of(rows[0], at[2]), lanes_of(rows[0], at[3])
            p12, p13 = lanes_of(rows[1], at[2]), lanes_of(rows[1], at[3])
            p22, p23, p33 = lanes_of(rows[2], at[2]), lanes_of(rows[2], at[3]), lanes_of(rows[3], at[3])
            scale = 1.0 / (a * c - b * b)
            row0 = jnp.where(low, one[0], rows[0])
            row1 = jnp.where(low, one[1], rows[1])
            turned0 = c * row0 - b * row1
            turned1 = a * row1 - b * row0
            g02, g12 = (c * p02 - b * p12) * scale, (a * p12 - b * p02) * scale
            g03, g13 = (c * p03 - b * p13) * scale, (a * p13 - b * p03) * scale
            s22 = p22 - (p02 * g02 + p12 * g12)
            s23 = p23 - (p02 * g03 + p12 * g13)
            s33 = p33 - (p03 * g03 + p13 * g13)
            row2 = jnp.where(low, 0.0, rows[2]) - (p02 * turned0 + p12 * turned1) * scale
            row3 = jnp.where(low, 0.0, rows[3]) - (p03 * turned0 + p13 * turned1) * scale
            again = 1.0 / (s22 * s33 - s23 * s23)
            row2 = jnp.where(high, one[2], row2)
            row3 = jnp.where(high, one[3], row3)
            turned2 = s33 * row2 - s23 * row3
            turned3 = s22 * row3 - s23 * row2
            for i in range(g, 8):
                f0, f1, f2, f3 = [lanes_of(groups[i], x) for x in at]
                new = jnp.where(low, 0.0, groups[i]) - (f0 * turned0 + f1 * turned1) * scale
                if i == g:
                    new = jnp.where(sub > s + 1, new, groups[i])
                groups[i] = new
                if i == g and s == 4:
                    continue
                f2 = f2 - (f0 * g02 + f1 * g12)
                f3 = f3 - (f0 * g03 + f1 * g13)
                new = jnp.where(high, 0.0, new) - (f2 * turned2 + f3 * turned3) * again
                groups[i] = jnp.where(sub > s + 3, new, groups[i]) if i == g else new
    odd = (sub & 1) == 1
    results = []
    for groups in pairs:
        outs = []
        logs = jnp.zeros((8, 128), F32)
        for i in range(8):
            row_id = sub + 8 * i
            diag = lanes_of(groups[i], half + row_id)
            side = lanes_of(groups[i], half + (row_id ^ 1))
            unit = jnp.where(col < row_id - (sub & 1), groups[i], (col == row_id).astype(F32))
            ratio = side / pltpu.roll(diag, 1, 0)
            unit = jnp.where(odd, unit - ratio * pltpu.roll(unit, 1, 0), unit)
            diag = jnp.where(odd, diag - ratio * side, diag)
            outs.append(unit * lax.rsqrt(diag))
            logs = logs + jnp.log(diag)
        results.append((outs, 0.5 * jnp.sum(logs, axis=0, keepdims=True)))
    return results


def spread_kernel(patterns_ref, out_ref):
    for z in range(8):
        out_ref[z] = patterns_ref[...]


def project_kernel(own_ref, other_ref, fields_ref, out_ref):
    core = lax.axis_index("core")
    parts = []
    for z in range(8):
        own, other = own_ref[z], other_ref[z]
        parts += [by_core(core, own, other), by_core(core, other, own)]
    patterns = jnp.concatenate(parts, axis=1)
    part = lax.dot_general(
        fields_ref[...], patterns, (((1,), (1,)), ((), ())), preferred_element_type=F32)
    days = part.shape[0] // 2
    part = jnp.concatenate([part[:days], part[days:]], axis=1).T
    for b in range(8):
        out_ref[2 * b] = part[8 * b:8 * b + 8]
        out_ref[2 * b + 1] = part[K + 8 * b:K + 8 * b + 8]


def read_pcs(pcs_ref):
    return [jnp.concatenate([pcs_ref[2 * b], pcs_ref[2 * b + 1]], axis=1) for b in range(8)]


def centre(pcs, shift):
    sub, _, _ = tile_ids()
    row = jnp.broadcast_to(jnp.concatenate([shift, shift], axis=1), (8, 128))
    outs = []
    for b in range(8):
        column = lanes_of(row, sub + 8 * b)
        outs.append(pcs[b] - jnp.concatenate([column] * (pcs[b].shape[1] // 128), axis=1))
    return jnp.concatenate(outs, axis=0)


def split(x):
    high = x.astype(BF16)
    rest = x - high.astype(F32)
    middle = rest.astype(BF16)
    return high, middle, (rest - middle.astype(F32)).astype(BF16)


def softmax_of(logp):
    top = jnp.max(logp, axis=0, keepdims=True)
    expo = jnp.exp(logp - top)
    return expo / jnp.sum(expo, axis=0, keepdims=True)


def moments(core, centred, terms, resp, keep_ref, send_ref):
    counts = jnp.broadcast_to(jnp.sum(resp, axis=1, keepdims=True), (R, K))
    row_id = lax.broadcasted_iota(jnp.int32, (K, K), 0)
    col_id = lax.broadcasted_iota(jnp.int32, (K, K), 1)
    left = jnp.concatenate([centred * resp[r:r + 1, :] for r in range(R)] + [resp], axis=0)
    high, middle, _ = split(left)
    contract = (((1,), (1,)), ((), ()))
    got = lax.dot_general(high, jnp.concatenate(terms, axis=0), contract, preferred_element_type=F32)
    more = lax.dot_general(middle, jnp.concatenate(terms[:2], axis=0), contract, preferred_element_type=F32)
    got = got[:, :K] + (got[:, K:2 * K] + more[:, :K]) + (got[:, 2 * K:] + more[:, K:])
    seconds = [got[K * r:K * r + K] for r in range(R)]
    firsts = [got[K * R + r:K * R + r + 1] for r in range(R)]
    packs = []
    for h in range(2):
        squares, tails = [], []
        for p in range(2):
            a = HALF * h + 2 * p
            squares.append(jnp.where(row_id >= col_id, seconds[a], seconds[a + 1]))
            diag = jnp.sum(jnp.where(row_id == col_id, seconds[a + 1], 0.0), axis=0, keepdims=True)
            tails.append(jnp.concatenate(
                [diag, firsts[a], firsts[a + 1], counts[a:a + 1], counts[a + 1:a + 2],
                 jnp.zeros((3, K), F32)], axis=0))
        packs.append(jnp.concatenate(
            [jnp.concatenate(squares, axis=1), jnp.concatenate(tails, axis=1)], axis=0))
    keep_ref[...] = by_core(core, packs[0], packs[1])
    send_ref[...] = by_core(core, packs[1], packs[0])


def put_shift(shift, shift_ref):
    shift_ref[...] = jnp.broadcast_to(jnp.concatenate([shift, shift], axis=1), (8, 128))


def first_kernel(pcs_ref, means_ref, variances_ref, mixing_ref, keep_ref, send_ref, shift_ref):
    pcs = read_pcs(pcs_ref)
    sub, _, _ = tile_ids()
    means, variances = means_ref[...], variances_ref[...]
    shift = jnp.sum(means, axis=0, keepdims=True) / R
    put_shift(shift, shift_ref)
    centred = centre(pcs, shift)
    params = jnp.concatenate([means - shift, 1.0 / variances], axis=1)
    mixing = jnp.zeros((R, 128), F32)
    for r in range(R):
        mixing = jnp.where(sub == r, mixing_ref[r], mixing)
    weights = mixing / jnp.sum(mixing, axis=0, keepdims=True)
    base = jnp.log(weights[:, 0:1]) - 0.5 * jnp.sum(jnp.log(variances), axis=1, keepdims=True)
    logs = []
    for r in range(R):
        row = jnp.broadcast_to(params[r:r + 1, :], (8, 128))
        total = None
        for b in range(8):
            mean = jnp.concatenate([lanes_of(row, sub + 8 * b)] * 8, axis=1)
            scale = jnp.concatenate([lanes_of(row, sub + (8 * b + K))] * 8, axis=1)
            apart = centred[8 * b:8 * b + 8] - mean
            term = apart * apart * scale
            total = term if total is None else total + term
        logs.append(jnp.sum(total, axis=0, keepdims=True))
    resp = softmax_of(base - 0.5 * jnp.concatenate(logs, axis=0))
    moments(lax.axis_index("core"), centred, split(centred), resp, keep_ref, send_ref)


def merge_kernel(parts_ref, shift_ref, block_ref):
    sub, half, col = tile_ids()
    total = parts_ref[0]
    for z in range(1, 8):
        total = total + parts_ref[z]
    packed = total[:K]
    flipped = packed.T
    flipped = jnp.concatenate([flipped[:K], flipped[K:]], axis=1)
    tail = total[K:]
    pairs = []
    infos = []
    for p in range(2):
        first, count, shift = tail[1 + p:2 + p], tail[3 + p:4 + p], shift_ref[0:1, :]
        counted = jnp.maximum(count, 1.0)
        mean = (first + count * shift) / counted
        delta = mean - shift
        rest = first - count * delta
        first_b, delta_b = jnp.broadcast_to(first, (8, 128)), jnp.broadcast_to(delta, (8, 128))
        scale = 1.0 / counted
        groups = []
        for g in range(8):
            row_id = sub + 8 * g
            straight, turned = packed[8 * g:8 * g + 8], flipped[8 * g:8 * g + 8]
            if p == 0:
                second = jnp.where(row_id >= col, straight, turned)
            else:
                second = jnp.where(row_id < col, straight, jnp.where(row_id > col, turned, tail[0:1]))
            at = half + row_id
            second = second - lanes_of(first_b, at) * delta - lanes_of(delta_b, at) * rest
            cov = second * scale + jnp.where(row_id == col, REG, 0.0)
            if block_ref.shape[0] > INFO + 8:
                at = INFO + 8 + K * p + 8 * g
                block_ref[at:at + 8, :] = cov
            groups.append(cov)
        pairs.append(groups)
        infos.append((mean, counted))
    (first_out, first_log), (second_out, second_log) = eliminate(pairs)
    for g in range(8):
        block_ref[8 * g:8 * g + 8, :] = first_out[g]
        block_ref[K + 8 * g:K + 8 * g + 8, :] = second_out[g]
    block_ref[INFO:INFO + 8, :] = jnp.concatenate(
        [infos[0][0], infos[1][0], first_log, second_log, infos[0][1], infos[1][1],
         jnp.zeros((2, 128), F32)], axis=0)


def regime_of(r):
    h, q = divmod(r, HALF)
    return h, q % 2, K * (q // 2)


def expect(pcs, halves):
    infos = [block[INFO:INFO + 8] for block in halves]

    def column(at):
        rows = []
        for r in range(R):
            h, p, offset = regime_of(r)
            rows.append(infos[h][at + p:at + p + 1, offset:offset + 1])
        return jnp.concatenate(rows, axis=0)

    means, inverses = [], []
    for r in range(R):
        h, p, offset = regime_of(r)
        means.append(infos[h][p:p + 1, offset:offset + K])
        inverses.append(halves[h][K * p:K * p + K, offset:offset + K])
    means = jnp.concatenate(means, axis=0)
    counted = column(4)
    weights = counted / jnp.sum(counted, axis=0, keepdims=True)
    shift = jnp.sum(means * weights, axis=0, keepdims=True)
    centred = centre(pcs, shift)
    days = centred.shape[1]
    apart = jnp.concatenate([means - shift, jnp.zeros((128 - R, K), F32)], axis=0).T
    terms = split(centred)
    ends = split(apart)
    c1, c2, c3 = [jnp.concatenate([x, y], axis=1) for x, y in zip(terms, ends)]
    w1, w2, w3 = split(jnp.concatenate(inverses, axis=0))
    left = jnp.concatenate([w1, w1, w2, w2, w1, w3], axis=1)
    right = jnp.concatenate([c1, c2, c1, c2, c3, c1], axis=0)
    shifted = jnp.dot(left, right, preferred_element_type=F32)
    logs = []
    for r in range(R):
        mine = shifted[K * r:K * r + K]
        mine = mine[:, :days] - mine[:, days + r:days + r + 1]
        logs.append(jnp.sum(mine * mine, axis=0, keepdims=True))
    logp = jnp.log(weights) - column(2) - 0.5 * jnp.concatenate(logs, axis=0)
    return softmax_of(logp), weights, means, shift, centred, terms


def halves_of(core, keep_ref, got_ref):
    keep, got = keep_ref[...], got_ref[...]
    return [by_core(core, keep, got), by_core(core, got, keep)]


def middle_kernel(pcs_ref, keep_ref, got_ref, out_keep_ref, out_send_ref, shift_ref):
    core = lax.axis_index("core")
    resp, _, _, shift, centred, terms = expect(read_pcs(pcs_ref), halves_of(core, keep_ref, got_ref))
    put_shift(shift, shift_ref)
    moments(core, centred, terms, resp, out_keep_ref, out_send_ref)


def last_kernel(pcs_ref, keep_ref, got_ref, fields_ref, member_ref, terms_ref, means_ref, covs_ref, weights_ref):
    core = lax.axis_index("core")
    halves = halves_of(core, keep_ref, got_ref)
    for r in range(R):
        h, p, offset = regime_of(r)
        at = INFO + 8 + K * p
        covs_ref[r] = halves[h][at:at + K, offset:offset + K]
    member, weights, means, _, _, _ = expect(read_pcs(pcs_ref), halves)
    member_ref[...] = member
    for r in range(R):
        weights_ref[r] = weights[r, 0]
    means_ref[...] = means
    count = jnp.broadcast_to(jnp.sum(member, axis=1, keepdims=True), (R, 128))
    rounded = member.astype(BF16)
    for j in range(16):
        terms_ref[j, :, 0:256] = jnp.dot(rounded, fields_ref[:, 256 * j:256 * j + 256], preferred_element_type=F32)
        terms_ref[j, :, 256:384] = count


def spread(x, n):
    return jnp.broadcast_to(x[None], (n,) + x.shape)


def merge(keep, send, shift, rows):
    half = keep + lax.ppermute(send, "core", SWAP)
    parts = lax.all_to_all(spread(half, 8), "z", 0, 0)
    block, = call(merge_kernel, [((rows, 128), F32)], [parts, shift], limit=SMALL, cost=COVER)
    return block, lax.ppermute(block, "core", SWAP)


def body(anomalies, eofs, means_init, variances, mixing):
    days = anomalies.shape[0]
    eight, = call(
        spread_kernel, [((8,) + eofs.shape, BF16)], [eofs], limit=SMALL,
        cost=COVER)
    own = lax.all_to_all(eight, "z", 0, 0)
    other = lax.ppermute(own, "core", SWAP)
    partial, = call(
        project_kernel, [((16, 8, days // 2), F32)], [own, other, anomalies], limit=SMALL)
    mine = jnp.sum(lax.all_to_all(partial, "grid", 0, 0), axis=0)
    pcs = lax.all_to_all(spread(mine, 16), "grid", 0, 0)

    pack = [((ROWS, 128), F32)] * 2 + [((8, 128), F32)]
    keep, send, shift = call(first_kernel, pack, [pcs, means_init, variances, mixing], scalars=1)
    block, got = merge(keep, send, shift, INFO + 8)
    keep, send, shift = call(middle_kernel, pack, [pcs, block, got])
    block, got = merge(keep, send, shift, INFO + 8 + 2 * K)
    member, terms, means, covs, weights = call(
        last_kernel,
        [((R, days), F32), ((16, R, 384), F32), ((R, K), F32), ((R, K, K), F32), ((R,), F32)],
        [pcs, block, got, anomalies], limit=SMALL, scalar_outs=1)
    sums = jnp.sum(lax.all_to_all(terms, ("z", "core"), 0, 0), axis=0)
    composites = (sums[:, :256] / jnp.maximum(sums[:, 256:257], 1.0)).astype(BF16)

    return (means, covs, weights, member, composites)


def solution(mesh):
    split = Mesh(mesh.devices.reshape(16, 8, 2), ("grid", "z", "core"))
    day = ("z", "core")
    in_specs = (P(day, "grid"), P(None, ("grid",) + day), P(), P(), P())
    out_specs = (P(), P(), P(), P(None, day), P(None, ("grid",) + day))
    return jax.shard_map(body, mesh=split, in_specs=in_specs, out_specs=out_specs, check_vma=False)
```

```python
import functools

import jax
import jax.numpy as jnp
from jax import lax
from jax.experimental import pallas as pl
from jax.experimental.pallas import tpu as pltpu
from jax.sharding import Mesh, PartitionSpec as P

K = 64
R = 8
HALF = R // 2
F32 = jnp.float32
BF16 = jnp.bfloat16
REG = 0.01
SWAP = [(0, 1), (1, 0)]
ROWS = K + 8
INFO = 2 * K
LIMIT = 48 * 1024 * 1024
SMALL = 16 * 1024 * 1024
COVER = pl.CostEstimate(flops=20 * 10 ** 10, transcendentals=0, bytes_accessed=0)
VMEM = pl.BlockSpec(memory_space=pltpu.VMEM)
SMEM = pl.BlockSpec(memory_space=pltpu.SMEM)


def call(kernel, outs, operands, limit=LIMIT, cost=None, scalars=0, scalar_outs=0):
    return pl.pallas_call(
        kernel,
        out_shape=tuple(jax.ShapeDtypeStruct(s, d) for s, d in outs),
        in_specs=[VMEM] * (len(operands) - scalars) + [SMEM] * scalars,
        out_specs=tuple([VMEM] * (len(outs) - scalar_outs) + [SMEM] * scalar_outs),
        compiler_params=pltpu.CompilerParams(vmem_limit_bytes=limit),
        cost_estimate=cost,
    )(*operands)


def lanes_of(x, index):
    return jnp.take_along_axis(x, index, axis=1)


def tile_ids():
    lane = lax.broadcasted_iota(jnp.int32, (8, 128), 1)
    sub = lax.broadcasted_iota(jnp.int32, (8, 128), 0)
    half = (lane >= K).astype(jnp.int32) * K
    return sub, half, lane - half


def by_core(core, at_zero, at_one):
    return jnp.where(core == 0, at_zero, at_one)


def eliminate(pairs):
    sub, half, col = tile_ids()
    for k in range(0, K, 4):
        g, s = divmod(k, 8)
        at = [half + (k + q) for q in range(4)]
        here = [col == k + q for q in range(4)]
        one = [h.astype(F32) for h in here]
        low, high = here[0] | here[1], here[2] | here[3]
        for groups in pairs:
            rows = [jnp.broadcast_to(groups[g][s + q:s + q + 1, :], (8, 128)) for q in range(4)]
            a, b, c = lanes_of(rows[0], at[0]), lanes_of(rows[0], at[1]), lanes_of(rows[1], at[1])
            p02, p03 = lanes_of(rows[0], at[2]), lanes_of(rows[0], at[3])
            p12, p13 = lanes_of(rows[1], at[2]), lanes_of(rows[1], at[3])
            p22, p23, p33 = lanes_of(rows[2], at[2]), lanes_of(rows[2], at[3]), lanes_of(rows[3], at[3])
            scale = 1.0 / (a * c - b * b)
            row0 = jnp.where(low, one[0], rows[0])
            row1 = jnp.where(low, one[1], rows[1])
            turned0 = c * row0 - b * row1
            turned1 = a * row1 - b * row0
            g02, g12 = (c * p02 - b * p12) * scale, (a * p12 - b * p02) * scale
            g03, g13 = (c * p03 - b * p13) * scale, (a * p13 - b * p03) * scale
            s22 = p22 - (p02 * g02 + p12 * g12)
            s23 = p23 - (p02 * g03 + p12 * g13)
            s33 = p33 - (p03 * g03 + p13 * g13)
            row2 = jnp.where(low, 0.0, rows[2]) - (p02 * turned0 + p12 * turned1) * scale
            row3 = jnp.where(low, 0.0, rows[3]) - (p03 * turned0 + p13 * turned1) * scale
            again = 1.0 / (s22 * s33 - s23 * s23)
            row2 = jnp.where(high, one[2], row2)
            row3 = jnp.where(high, one[3], row3)
            turned2 = s33 * row2 - s23 * row3
            turned3 = s22 * row3 - s23 * row2
            for i in range(g, 8):
                f0, f1, f2, f3 = [lanes_of(groups[i], x) for x in at]
                new = jnp.where(low, 0.0, groups[i]) - (f0 * turned0 + f1 * turned1) * scale
                if i == g:
                    new = jnp.where(sub > s + 1, new, groups[i])
                groups[i] = new
                if i == g and s == 4:
                    continue
                f2 = f2 - (f0 * g02 + f1 * g12)
                f3 = f3 - (f0 * g03 + f1 * g13)
                new = jnp.where(high, 0.0, new) - (f2 * turned2 + f3 * turned3) * again
                groups[i] = jnp.where(sub > s + 3, new, groups[i]) if i == g else new
    odd = (sub & 1) == 1
    results = []
    for groups in pairs:
        outs = []
        logs = jnp.zeros((8, 128), F32)
        for i in range(8):
            row_id = sub + 8 * i
            diag = lanes_of(groups[i], half + row_id)
            side = lanes_of(groups[i], half + (row_id ^ 1))
            unit = jnp.where(col < row_id - (sub & 1), groups[i], (col == row_id).astype(F32))
            ratio = side / pltpu.roll(diag, 1, 0)
            unit = jnp.where(odd, unit - ratio * pltpu.roll(unit, 1, 0), unit)
            diag = jnp.where(odd, diag - ratio * side, diag)
            outs.append(unit * lax.rsqrt(diag))
            logs = logs + jnp.log(diag)
        results.append((outs, 0.5 * jnp.sum(logs, axis=0, keepdims=True)))
    return results


def spread_kernel(patterns_ref, out_ref):
    for z in range(8):
        out_ref[z] = patterns_ref[...]


def project_kernel(own_ref, other_ref, fields_ref, out_ref):
    core = lax.axis_index("core")
    parts = []
    for z in range(8):
        own, other = own_ref[z], other_ref[z]
        parts += [by_core(core, own, other), by_core(core, other, own)]
    patterns = jnp.concatenate(parts, axis=1)
    part = lax.dot_general(
        fields_ref[...], patterns, (((1,), (1,)), ((), ())), preferred_element_type=F32)
    days = part.shape[0] // 2
    part = jnp.concatenate([part[:days], part[days:]], axis=1).T
    for b in range(8):
        out_ref[2 * b] = part[8 * b:8 * b + 8]
        out_ref[2 * b + 1] = part[K + 8 * b:K + 8 * b + 8]


def read_pcs(pcs_ref):
    return [jnp.concatenate([pcs_ref[2 * b], pcs_ref[2 * b + 1]], axis=1) for b in range(8)]


def centre(pcs, shift):
    sub, _, _ = tile_ids()
    row = jnp.broadcast_to(jnp.concatenate([shift, shift], axis=1), (8, 128))
    outs = []
    for b in range(8):
        column = lanes_of(row, sub + 8 * b)
        outs.append(pcs[b] - jnp.concatenate([column] * (pcs[b].shape[1] // 128), axis=1))
    return jnp.concatenate(outs, axis=0)


def split(x):
    high = x.astype(BF16)
    rest = x - high.astype(F32)
    middle = rest.astype(BF16)
    return high, middle, (rest - middle.astype(F32)).astype(BF16)


def softmax_of(logp):
    top = jnp.max(logp, axis=0, keepdims=True)
    expo = jnp.exp(logp - top)
    return expo / jnp.sum(expo, axis=0, keepdims=True)


def moments(core, centred, terms, resp, keep_ref, send_ref):
    counts = jnp.broadcast_to(jnp.sum(resp, axis=1, keepdims=True), (R, K))
    row_id = lax.broadcasted_iota(jnp.int32, (K, K), 0)
    col_id = lax.broadcasted_iota(jnp.int32, (K, K), 1)
    left = jnp.concatenate([centred * resp[r:r + 1, :] for r in range(R)] + [resp], axis=0)
    high, middle, _ = split(left)
    contract = (((1,), (1,)), ((), ()))
    got = lax.dot_general(high, jnp.concatenate(terms, axis=0), contract, preferred_element_type=F32)
    more = lax.dot_general(middle, jnp.concatenate(terms[:2], axis=0), contract, preferred_element_type=F32)
    got = got[:, :K] + (got[:, K:2 * K] + more[:, :K]) + (got[:, 2 * K:] + more[:, K:])
    seconds = [got[K * r:K * r + K] for r in range(R)]
    firsts = [got[K * R + r:K * R + r + 1] for r in range(R)]
    packs = []
    for h in range(2):
        squares, tails = [], []
        for p in range(2):
            a = HALF * h + 2 * p
            squares.append(jnp.where(row_id >= col_id, seconds[a], seconds[a + 1]))
            diag = jnp.sum(jnp.where(row_id == col_id, seconds[a + 1], 0.0), axis=0, keepdims=True)
            tails.append(jnp.concatenate(
                [diag, firsts[a], firsts[a + 1], counts[a:a + 1], counts[a + 1:a + 2],
                 jnp.zeros((3, K), F32)], axis=0))
        packs.append(jnp.concatenate(
            [jnp.concatenate(squares, axis=1), jnp.concatenate(tails, axis=1)], axis=0))
    keep_ref[...] = by_core(core, packs[0], packs[1])
    send_ref[...] = by_core(core, packs[1], packs[0])


def put_shift(shift, shift_ref):
    shift_ref[...] = jnp.broadcast_to(jnp.concatenate([shift, shift], axis=1), (8, 128))


def first_kernel(pcs_ref, means_ref, variances_ref, mixing_ref, keep_ref, send_ref, shift_ref):
    pcs = read_pcs(pcs_ref)
    sub, _, _ = tile_ids()
    means, variances = means_ref[...], variances_ref[...]
    shift = jnp.sum(means, axis=0, keepdims=True) / R
    put_shift(shift, shift_ref)
    centred = centre(pcs, shift)
    params = jnp.concatenate([means - shift, 1.0 / variances], axis=1)
    mixing = jnp.zeros((R, 128), F32)
    for r in range(R):
        mixing = jnp.where(sub == r, mixing_ref[r], mixing)
    weights = mixing / jnp.sum(mixing, axis=0, keepdims=True)
    base = jnp.log(weights[:, 0:1]) - 0.5 * jnp.sum(jnp.log(variances), axis=1, keepdims=True)
    logs = []
    for r in range(R):
        row = jnp.broadcast_to(params[r:r + 1, :], (8, 128))
        total = None
        for b in range(8):
            mean = jnp.concatenate([lanes_of(row, sub + 8 * b)] * 8, axis=1)
            scale = jnp.concatenate([lanes_of(row, sub + (8 * b + K))] * 8, axis=1)
            apart = centred[8 * b:8 * b + 8] - mean
            term = apart * apart * scale
            total = term if total is None else total + term
        logs.append(jnp.sum(total, axis=0, keepdims=True))
    resp = softmax_of(base - 0.5 * jnp.concatenate(logs, axis=0))
    moments(lax.axis_index("core"), centred, split(centred), resp, keep_ref, send_ref)


def merge_kernel(parts_ref, shift_ref, block_ref):
    sub, half, col = tile_ids()
    total = parts_ref[0]
    for z in range(1, 8):
        total = total + parts_ref[z]
    packed = total[:K]
    flipped = packed.T
    flipped = jnp.concatenate([flipped[:K], flipped[K:]], axis=1)
    tail = total[K:]
    pairs = []
    infos = []
    for p in range(2):
        first, count, shift = tail[1 + p:2 + p], tail[3 + p:4 + p], shift_ref[0:1, :]
        counted = jnp.maximum(count, 1.0)
        mean = (first + count * shift) / counted
        delta = mean - shift
        rest = first - count * delta
        first_b, delta_b = jnp.broadcast_to(first, (8, 128)), jnp.broadcast_to(delta, (8, 128))
        scale = 1.0 / counted
        groups = []
        for g in range(8):
            row_id = sub + 8 * g
            straight, turned = packed[8 * g:8 * g + 8], flipped[8 * g:8 * g + 8]
            if p == 0:
                second = jnp.where(row_id >= col, straight, turned)
            else:
                second = jnp.where(row_id < col, straight, jnp.where(row_id > col, turned, tail[0:1]))
            at = half + row_id
            second = second - lanes_of(first_b, at) * delta - lanes_of(delta_b, at) * rest
            cov = second * scale + jnp.where(row_id == col, REG, 0.0)
            if block_ref.shape[0] > INFO + 8:
                at = INFO + 8 + K * p + 8 * g
                block_ref[at:at + 8, :] = cov
            groups.append(cov)
        pairs.append(groups)
        infos.append((mean, counted))
    (first_out, first_log), (second_out, second_log) = eliminate(pairs)
    for g in range(8):
        block_ref[8 * g:8 * g + 8, :] = first_out[g]
        block_ref[K + 8 * g:K + 8 * g + 8, :] = second_out[g]
    block_ref[INFO:INFO + 8, :] = jnp.concatenate(
        [infos[0][0], infos[1][0], first_log, second_log, infos[0][1], infos[1][1],
         jnp.zeros((2, 128), F32)], axis=0)


def regime_of(r):
    h, q = divmod(r, HALF)
    return h, q % 2, K * (q // 2)


def expect(pcs, halves):
    infos = [block[INFO:INFO + 8] for block in halves]

    def column(at):
        rows = []
        for r in range(R):
            h, p, offset = regime_of(r)
            rows.append(infos[h][at + p:at + p + 1, offset:offset + 1])
        return jnp.concatenate(rows, axis=0)

    means, inverses = [], []
    for r in range(R):
        h, p, offset = regime_of(r)
        means.append(infos[h][p:p + 1, offset:offset + K])
        inverses.append(halves[h][K * p:K * p + K, offset:offset + K])
    means = jnp.concatenate(means, axis=0)
    counted = column(4)
    weights = counted / jnp.sum(counted, axis=0, keepdims=True)
    shift = jnp.sum(means * weights, axis=0, keepdims=True)
    centred = centre(pcs, shift)
    days = centred.shape[1]
    apart = jnp.concatenate([means - shift, jnp.zeros((128 - R, K), F32)], axis=0).T
    terms = split(centred)
    ends = split(apart)
    c1, c2, c3 = [jnp.concatenate([x, y], axis=1) for x, y in zip(terms, ends)]
    w1, w2, w3 = split(jnp.concatenate(inverses, axis=0))
    left = jnp.concatenate([w1, w1, w2, w2, w1, w3], axis=1)
    right = jnp.concatenate([c1, c2, c1, c2, c3, c1], axis=0)
    shifted = jnp.dot(left, right, preferred_element_type=F32)
    logs = []
    for r in range(R):
        mine = shifted[K * r:K * r + K]
        mine = mine[:, :days] - mine[:, days + r:days + r + 1]
        logs.append(jnp.sum(mine * mine, axis=0, keepdims=True))
    logp = jnp.log(weights) - column(2) - 0.5 * jnp.concatenate(logs, axis=0)
    return softmax_of(logp), weights, means, shift, centred, terms


def halves_of(core, keep_ref, got_ref):
    keep, got = keep_ref[...], got_ref[...]
    return [by_core(core, keep, got), by_core(core, got, keep)]


def middle_kernel(pcs_ref, keep_ref, got_ref, out_keep_ref, out_send_ref, shift_ref):
    core = lax.axis_index("core")
    resp, _, _, shift, centred, terms = expect(read_pcs(pcs_ref), halves_of(core, keep_ref, got_ref))
    put_shift(shift, shift_ref)
    moments(core, centred, terms, resp, out_keep_ref, out_send_ref)


def last_kernel(pcs_ref, keep_ref, got_ref, fields_ref, member_ref, stay_ref, send_ref, means_ref, covs_ref, weights_ref):
    core = lax.axis_index("core")
    halves = halves_of(core, keep_ref, got_ref)
    for r in range(R):
        h, p, offset = regime_of(r)
        at = INFO + 8 + K * p
        covs_ref[r] = halves[h][at:at + K, offset:offset + K]
    member, weights, means, _, _, _ = expect(read_pcs(pcs_ref), halves)
    member_ref[...] = member
    for r in range(R):
        weights_ref[r] = weights[r, 0]
    means_ref[...] = means
    count = jnp.broadcast_to(jnp.sum(member, axis=1, keepdims=True), (R, 128))
    rounded = member.astype(BF16)
    for z in range(8):
        both = jnp.dot(rounded, fields_ref[:, 512 * z:512 * z + 512], preferred_element_type=F32)
        stay_ref[z, :, 0:256] = by_core(core, both[:, :256], both[:, 256:])
        send_ref[z, :, 0:256] = by_core(core, both[:, 256:], both[:, :256])
        stay_ref[z, :, 256:384] = count
        send_ref[z, :, 256:384] = count


def spread(x, n):
    return jnp.broadcast_to(x[None], (n,) + x.shape)


def merge(keep, send, shift, rows):
    half = keep + lax.ppermute(send, "core", SWAP)
    parts = lax.all_to_all(spread(half, 8), "z", 0, 0)
    block, = call(merge_kernel, [((rows, 128), F32)], [parts, shift], limit=SMALL, cost=COVER)
    return block, lax.ppermute(block, "core", SWAP)


def body(anomalies, eofs, means_init, variances, mixing):
    days = anomalies.shape[0]
    eight, = call(
        spread_kernel, [((8,) + eofs.shape, BF16)], [eofs], limit=SMALL,
        cost=COVER)
    own = lax.all_to_all(eight, "z", 0, 0)
    other = lax.ppermute(own, "core", SWAP)
    partial, = call(
        project_kernel, [((16, 8, days // 2), F32)], [own, other, anomalies], limit=SMALL)
    mine = jnp.sum(lax.all_to_all(partial, "grid", 0, 0), axis=0)
    pcs = lax.all_to_all(spread(mine, 16), "grid", 0, 0)

    pack = [((ROWS, 128), F32)] * 2 + [((8, 128), F32)]
    keep, send, shift = call(first_kernel, pack, [pcs, means_init, variances, mixing], scalars=1)
    block, got = merge(keep, send, shift, INFO + 8)
    keep, send, shift = call(middle_kernel, pack, [pcs, block, got])
    block, got = merge(keep, send, shift, INFO + 8 + 2 * K)
    member, stay, send, means, covs, weights = call(
        last_kernel,
        [((R, days), F32), ((8, R, 384), F32), ((8, R, 384), F32), ((R, K), F32), ((R, K, K), F32), ((R,), F32)],
        [pcs, block, got, anomalies], limit=SMALL, scalar_outs=1)
    sums = jnp.sum(lax.all_to_all(stay + lax.ppermute(send, "core", SWAP), "z", 0, 0), axis=0)
    composites = (sums[:, :256] / jnp.maximum(sums[:, 256:257], 1.0)).astype(BF16)

    return (means, covs, weights, member, composites)


def solution(mesh):
    split = Mesh(mesh.devices.reshape(16, 8, 2), ("grid", "z", "core"))
    day = ("z", "core")
    in_specs = (P(day, "grid"), P(None, ("grid",) + day), P(), P(), P())
    out_specs = (P(), P(), P(), P(None, day), P(None, ("grid",) + day))
    return jax.shard_map(body, mesh=split, in_specs=in_specs, out_specs=out_specs, check_vma=False)
```
